32 devices in a mesh: tile: 8 (over y, x, core), sect: 2 (over z_hi), lev: 2 (over z_lo).
Axes of the slice: x: 2, y: 2, z: 4 (z_hi: 2, z_lo: 2; z = z_hi * 2 + z_lo), core: 2. Of those that a mesh axis runs over, the one named last changes fastest.
Arguments:
- adjoint: float32 [2, 8, 64, 128, 128], P('sect', 'tile', 'lev'), may hold values from -6 to 6
- diffusion: float32 [2, 8, 128, 128], P('sect', 'tile'), may hold values from 0.02 to 0.12
- wet_mask: int32 [2, 8, 128, 128], P('sect', 'tile'), may hold values 0 or 1
- remap: int32 [2, 8, 128], P('sect', 'tile'), may hold values from 0 to 127
- coupling: float32 [2, 64], P('sect', 'lev'), may hold values from 0.1 to 0.5
- vert_inverse: float32 [2, 8, 64, 64], P('sect', 'tile')
- nbr_tile: int32 [8, 4], P('tile'), may hold values from -1 to 7, as said below
- nbr_side: int32 [8, 4], P('tile'), may hold values from 0 to 3
- nbr_flip: int32 [8, 4], P('tile'), may hold values from 0 to 1
Outputs:
- result: float32 [2, 8, 64, 128, 128], P('sect', 'tile', 'lev')
The draws below stay inside these ranges and needn't reach their ends.
Inputs may be any that keep to these rules, and one draw needn't show every extreme that they name: `nbr_tile`: A side with a neighbour is named back by that neighbour's named side with the same flip.
All inputs are finite; a program needn't handle non-finite values. No bound on the sum of `wet_mask` on one device may be relied on, other than what follows from the above.
Results may differ from the reference program's by a relative error of at most 0.0001.
Values sent between devices are 32-bit elements; how exact they have to be, the bound alone decides.
No kernel may reach another device: no remote copies, remote signals or barrier semaphores. Data moves between devices by JAX's collectives and lax.ppermute only.
A program may use at most 64 MiB of HBM per device.

```python
import math
import jax
import jax.numpy as jnp
from jax import lax

C = 128
LEV = 64
TILES = 8


def neighbour_table(key):
    base = jax.random.fold_in(key, 11)
    slots = TILES * 4
    order = jax.random.permutation(jax.random.fold_in(base, 1), slots).astype(jnp.int32)
    pairs = order.reshape(-1, 2)
    pair_count = slots // 2
    flips = jax.random.randint(jax.random.fold_in(base, 2), (pair_count,), 0, 2).astype(jnp.int32)
    alive = (jnp.arange(pair_count) >= pair_count // 8).astype(jnp.int32)
    empty = jnp.zeros((slots,), jnp.int32)
    partner = empty.at[pairs[:, 0]].set(pairs[:, 1]).at[pairs[:, 1]].set(pairs[:, 0])
    slot_alive = empty.at[pairs[:, 0]].set(alive).at[pairs[:, 1]].set(alive)
    slot_flip = empty.at[pairs[:, 0]].set(flips * alive).at[pairs[:, 1]].set(flips * alive)
    tiles = jnp.where(slot_alive == 1, partner // 4, -1).astype(jnp.int32)
    sides = jnp.where(slot_alive == 1, partner % 4, 0).astype(jnp.int32)
    return (tiles.reshape(TILES, 4), sides.reshape(TILES, 4), slot_flip.reshape(TILES, 4))


def draw_nbr_tile(key, part):
    return neighbour_table(key)[0]


def draw_nbr_side(key, part):
    return neighbour_table(key)[1]


def draw_nbr_flip(key, part):
    return neighbour_table(key)[2]


def draw_vert_inverse(key, part):
    shape = (2, TILES, LEV, LEV)
    noise = jax.random.normal(key, shape, jnp.float32)
    return jnp.eye(LEV, dtype=jnp.float32) + noise * (0.5 / math.sqrt(LEV))


def place_ends(array, own_key, low, largest):
    spot = [jax.random.randint(jax.random.fold_in(own_key, axis), (), 0, length) for axis, length in enumerate(array.shape)]
    widest = array.shape.index(max(array.shape))
    next_to = spot[:widest] + [(spot[widest] + 1) % array.shape[widest]] + spot[widest + 1:]
    return array.at[tuple(spot)].set(low).at[tuple(next_to)].set(largest)


def block_scale(stream_key, shape, shards, smallest, largest):
    loudness = 1.0
    for axis_at, blocks in shards:
        steps = jax.random.uniform(jax.random.fold_in(jax.random.fold_in(stream_key, 6), axis_at), (blocks,), jnp.float32, smallest / len(shards), largest / len(shards))
        loudness = loudness * jnp.repeat(jnp.exp(steps), shape[axis_at] // blocks).reshape((-1,) + (1,) * (len(shape) - 1 - axis_at))
    return loudness


def gaussian(stream_key, extent, width, bound, split=(), kind=jnp.bfloat16):
    entries = width * jax.random.normal(stream_key, extent, jnp.float32)
    if split:
        entries = entries * block_scale(stream_key, extent, split, -0.22, 0.18)
    return jnp.clip(entries, -bound, bound).astype(kind)


def setup_inputs(seed: int = 0) -> dict:
    streams_of = jax.random.split(jax.random.key(seed), 10)
    return {
        "adjoint": gaussian(streams_of[0], (2, TILES, LEV, C, C), 1.0, 6.0, ((0, 2), (1, 8), (2, 2)), jnp.float32),
        "diffusion": jnp.clip(jnp.exp(math.log(0.12) - 1.7917595 * jax.random.uniform(streams_of[1], (2, TILES, C, C), jnp.float32) ** block_scale(streams_of[1], (2, TILES, C, C), ((0, 2), (1, 8)), -0.2, 0.2)), 0.02, 0.12),
        "wet_mask": place_ends((jax.random.randint(streams_of[2], (2, TILES, C, C), 0, 8) < 7).astype(jnp.int32), jax.random.fold_in(streams_of[2], 1), 0, 1),
        "remap": place_ends(jax.random.randint(streams_of[3], (2, TILES, C), 0, C), jax.random.fold_in(streams_of[3], 1), 0, C - 1).astype(jnp.int32),
        "coupling": jnp.clip(jnp.exp(math.log(0.5) - 1.609438 * jax.random.uniform(streams_of[4], (2, LEV), jnp.float32) ** block_scale(streams_of[4], (2, LEV), ((0, 2), (1, 2)), -0.2, 0.2)), 0.1, 0.5),
        "vert_inverse": draw_vert_inverse(jax.random.fold_in(streams_of[9], 71), 0),
        "nbr_tile": draw_nbr_tile(jax.random.fold_in(streams_of[9], 71), 0),
        "nbr_side": draw_nbr_side(jax.random.fold_in(streams_of[9], 71), 0),
        "nbr_flip": draw_nbr_flip(jax.random.fold_in(streams_of[9], 71), 0),
    }


def edge_rows(field):
    return jnp.stack([field[..., 0, :], field[..., -1, :], field[..., :, 0], field[..., :, -1]], axis=-3)


def halo_from(all_edges, tiles, sides, flips):
    picked = all_edges[jnp.maximum(tiles, 0), sides]
    turned = jnp.where((flips == 1)[:, :, None, None], picked[..., ::-1], picked)
    return jnp.where((tiles >= 0)[:, :, None, None], turned, jnp.float32(0.0))


def laplace(field, halo):
    upper = jnp.concatenate([halo[:, 0][:, :, None, :], field[:, :, :-1, :]], axis=2)
    lower = jnp.concatenate([field[:, :, 1:, :], halo[:, 1][:, :, None, :]], axis=2)
    left_side = jnp.concatenate([halo[:, 2][:, :, :, None], field[:, :, :, :-1]], axis=3)
    right_side = jnp.concatenate([field[:, :, :, 1:], halo[:, 3][:, :, :, None]], axis=3)
    return upper + lower + left_side + right_side - 4.0 * field


def pick_tile_rows(field, rows):
    return field[:, rows, :]


def reference(adjoint, diffusion, wet_mask, remap, coupling, vert_inverse, nbr_tile, nbr_side, nbr_flip):
    wet_cells = wet_mask.astype(jnp.float32)
    current = adjoint
    for step in range(2):
        partner = current[::-1]
        pulled = jax.vmap(jax.vmap(pick_tile_rows))(partner, remap)
        coupled = current + coupling[:, None, :, None, None] * pulled
        column = jnp.einsum("ctkl,ctkxy->ctlxy", vert_inverse, coupled, precision=lax.Precision.HIGHEST)
        flux = wet_cells[:, :, None] * diffusion[:, :, None] * column
        outputs = []
        for component in range(2):
            halo = halo_from(edge_rows(flux[component]), nbr_tile, nbr_side, nbr_flip)
            outputs.append(wet_cells[component][:, None] * (column[component] + laplace(flux[component], halo)))
        current = jnp.stack(outputs)
    return current
```

```python
import jax
import jax.numpy as jnp
from jax import lax
from jax.experimental import pallas as pl
from jax.experimental.pallas import tpu as pltpu
from jax.sharding import PartitionSpec as P

Z = ("sect", "lev")
PARTS = 4
HIGHEST = lax.Precision.HIGHEST


def exchanged(block, bits):
    return lax.ppermute(block, Z, [(at, at ^ bits) for at in range(PARTS)])


def split_kernel(place, field, *outs_and_scratch):
    outs, turned = outs_and_scratch[:PARTS], outs_and_scratch[PARTS]
    levels, rows, cols = field.shape
    width = cols // PARTS
    zero = jnp.zeros((levels, rows), jnp.float32)
    turned[0:levels, :] = zero
    turned[(cols + 1) * levels : (cols + 2) * levels, :] = zero
    for level in range(levels):
        turned[pl.ds(levels + level, cols, stride=levels), :] = field[level].T
    for bits, out in enumerate(outs):
        first = (place[0] ^ bits) * (width * levels)
        out[...] = turned[pl.ds(pl.multiple_of(first, 8), (width + 2) * levels), :].reshape(out.shape)


def split_columns(field, place):
    levels, rows, cols = field.shape
    part = jax.ShapeDtypeStruct((cols // PARTS + 2, levels, rows), jnp.float32)
    return pl.pallas_call(
        split_kernel,
        out_shape=[part] * PARTS,
        in_specs=[
            pl.BlockSpec(memory_space=pltpu.SMEM),
            pl.BlockSpec(memory_space=pltpu.VMEM),
        ],
        out_specs=[pl.BlockSpec(memory_space=pltpu.VMEM)] * PARTS,
        scratch_shapes=[pltpu.VMEM(((cols + 2) * levels, rows), jnp.float32)],
        name="split_columns",
    )(place, field)


def join_kernel(place, p0, p1, p2, p3, sides, top_bottom, out, turned):
    levels, rows, cols = out.shape
    width = cols // PARTS
    for bits, part in enumerate((p0, p1, p2, p3)):
        first = (place[0] ^ bits) * (width * levels)
        turned[pl.ds(pl.multiple_of(first, 8), width * levels), :] = part[...].reshape(width * levels, rows)
    for part in range(PARTS):
        for side in range(2):
            at = (part * width + side * (width - 1)) * levels
            turned[at : at + levels, :] = turned[at : at + levels, :] + sides[part, side]
    row = lax.broadcasted_iota(jnp.int32, (rows, cols), 0)
    for level in range(levels):
        plane = turned[pl.ds(level, cols, stride=levels), :].T
        top = top_bottom[0, level : level + 1, :]
        bottom = top_bottom[1, level : level + 1, :]
        out[level] = plane + jnp.where(row == 0, top, jnp.where(row == rows - 1, bottom, 0.0))


def join_columns(parts, place, sides, top_bottom):
    width, levels, rows = parts[0].shape
    cols = width * PARTS
    return pl.pallas_call(
        join_kernel,
        out_shape=jax.ShapeDtypeStruct((levels, rows, cols), jnp.float32),
        in_specs=[pl.BlockSpec(memory_space=pltpu.SMEM)] + [pl.BlockSpec(memory_space=pltpu.VMEM)] * 6,
        out_specs=pl.BlockSpec(memory_space=pltpu.VMEM),
        scratch_shapes=[pltpu.VMEM((cols * levels, rows), jnp.float32)],
        name="join_columns",
    )(place, *parts, sides, top_bottom)


def halves(value):
    high = value.astype(jnp.bfloat16)
    low = (value - high.astype(jnp.float32)).astype(jnp.bfloat16)
    return high, low


def steps_kernel(
    place, x0, x1, x2, x3, weights, gains, rows_from, wet, spread, h0, h1, h2, h3,
    r0, r1, r2, r3, e0, e1, e2, e3, column, flux, state,
):
    ins, halos, outs, edges = (x0, x1, x2, x3), (h0, h1, h2, h3), (r0, r1, r2, r3), (e0, e1, e2, e3)
    width, half, rows = r0.shape
    levels = 2 * half
    lane = lax.broadcasted_iota(jnp.int32, (levels, rows), 1)
    mixes, picks = [], []
    for comp in range(2):
        high, low = halves(weights[comp])
        mixes.append(jnp.concatenate([high, low, high], axis=1))
        picks.append(jnp.broadcast_to(rows_from[comp : comp + 1, :], (levels, rows)))

    def picked(value, index):
        return jnp.take_along_axis(value, index, axis=1, mode="promise_in_bounds")

    def solve(blocks, at):
        for comp in range(2):
            rights = []
            for block in blocks:
                coupled = block[comp] + gains[comp] * picked(block[1 - comp], picks[comp])
                high, low = halves(coupled)
                rights.append(jnp.concatenate([high, high, low], axis=0))
            solved = jnp.dot(
                mixes[comp], jnp.concatenate(rights, axis=1), preferred_element_type=jnp.float32
            )
            for b in range(len(blocks)):
                one = solved[:, b * rows : (b + 1) * rows]
                column[comp, at + b] = one
                flux[comp, at + b] = one * spread[comp, pl.ds(at + b, 1), :]

    def first_solve(pair, carry):
        at = 2 * pair
        blocks = []
        for b in range(2):
            blocks.append(
                [jnp.concatenate([ins[2 * c][at + b], ins[2 * c + 1][at + b]], axis=0) for c in range(2)]
            )
        solve(blocks, at)
        return carry

    lax.fori_loop(0, (width + 2) // 2, first_solve, 0)

    def side(comp, slot):
        return jnp.concatenate([halos[2 * comp][slot], halos[2 * comp + 1][slot]], axis=0)

    @pl.when(place[0] == 0)
    def _():
        for comp in range(2):
            flux[comp, 0] = side(comp, 0)

    @pl.when(place[0] == PARTS - 1)
    def _():
        for comp in range(2):
            flux[comp, width + 1] = side(comp, 0)

    ends = [side(comp, 1) for comp in range(2)]

    def first_spread(j, carry):
        for comp in range(2):
            mid = flux[comp, j + 1]
            above = jnp.where(lane == 0, picked(ends[comp], jnp.full((levels, rows), j)), pltpu.roll(mid, 1, 1))
            below = jnp.where(
                lane == rows - 1,
                picked(ends[comp], jnp.full((levels, rows), j + width)),
                pltpu.roll(mid, rows - 1, 1),
            )
            total = above + below + flux[comp, j] + flux[comp, j + 2] - 4.0 * mid
            state[comp, j] = wet[comp, pl.ds(j + 1, 1), :] * (column[comp, j + 1] + total)
        return carry

    lax.fori_loop(0, width, first_spread, 0)

    def second_solve(pair, carry):
        at = 2 * pair
        solve([[state[c, at + b] for c in range(2)] for b in range(2)], at + 1)
        return carry

    lax.fori_loop(0, width // 2, second_solve, 0)
    for comp in range(2):
        flux[comp, 0] = jnp.zeros((levels, rows), jnp.float32)
        flux[comp, width + 1] = jnp.zeros((levels, rows), jnp.float32)

    def second_spread(j, carry):
        kept = []
        for comp in range(2):
            mid = flux[comp, j + 1]
            above = jnp.where(lane == 0, 0.0, pltpu.roll(mid, 1, 1))
            below = jnp.where(lane == rows - 1, 0.0, pltpu.roll(mid, rows - 1, 1))
            total = above + below + flux[comp, j] + flux[comp, j + 2] - 4.0 * mid
            done = wet[comp, pl.ds(j + 1, 1), :] * (column[comp, j + 1] + total)
            outs[2 * comp][j] = done[:half]
            outs[2 * comp + 1][j] = done[half:]
            top = picked(mid, jnp.zeros((levels, rows), jnp.int32))
            bottom = picked(mid, jnp.full((levels, rows), rows - 1))
            kept.append(jnp.where(lane == j, top, jnp.where(lane == j + width, bottom, carry[comp])))
        return tuple(kept)

    empty = jnp.zeros((levels, rows), jnp.float32)
    tops = lax.fori_loop(0, width, second_spread, (empty, empty))
    for comp in range(2):
        for part in range(2):
            edge = edges[2 * comp + part]
            span = slice(part * half, (part + 1) * half)
            edge[0] = flux[comp, 1, span, :]
            edge[1] = flux[comp, width, span, :]
            edge[2] = tops[comp][span]


def two_steps(place, parts, weights, gains, rows_from, wet, spread, halos):
    wide, half, rows = parts[0].shape
    width = wide - 2
    part = jax.ShapeDtypeStruct((width, half, rows), jnp.float32)
    edge = jax.ShapeDtypeStruct((3, half, rows), jnp.float32)
    outs = pl.pallas_call(
        steps_kernel,
        out_shape=[part] * PARTS + [edge] * PARTS,
        in_specs=[pl.BlockSpec(memory_space=pltpu.SMEM)] + [pl.BlockSpec(memory_space=pltpu.VMEM)] * 13,
        out_specs=[pl.BlockSpec(memory_space=pltpu.VMEM)] * (2 * PARTS),
        scratch_shapes=[
            pltpu.VMEM((2, wide, 2 * half, rows), jnp.float32),
            pltpu.VMEM((2, wide, 2 * half, rows), jnp.float32),
            pltpu.VMEM((2, width, 2 * half, rows), jnp.float32),
        ],
        name="two_steps",
    )(place, *parts, weights, gains, rows_from, wet, spread, *halos)
    return outs[:PARTS], outs[PARTS:]


def tile_halo(edges, nbr_tile, nbr_side, nbr_flip):
    every = lax.all_gather(edges, "tile", axis=0)
    picked = every[jnp.maximum(nbr_tile, 0), nbr_side]
    turned = jnp.where((nbr_flip == 1)[:, None, None], picked[..., ::-1], picked)
    return jnp.where((nbr_tile >= 0)[:, None, None], turned, jnp.float32(0.0))


def on_device(
    adjoint, diffusion, wet_mask, remap, coupling, vert_inverse, nbr_tile, nbr_side, nbr_flip
):
    field = adjoint[0, 0]
    half, rows, cols = field.shape
    width = cols // PARTS
    level_at = lax.axis_index("lev")
    spot = lax.axis_index("sect") * 2 + level_at
    place = spot[None].astype(jnp.int32)
    wet = wet_mask[0, 0].astype(jnp.float32)
    spread = wet * diffusion[0, 0]
    near = (nbr_tile[0], nbr_side[0], nbr_flip[0])

    parts = split_columns(field, place)
    arrived = [parts[0]] + [exchanged(parts[bits], bits) for bits in range(1, PARTS)]

    order = vert_inverse[0, 0]
    order = jnp.where(level_at == 0, order, jnp.roll(order, half, axis=0))
    order = jnp.where(level_at == 0, order, jnp.roll(order, half, axis=1))
    gain = jnp.concatenate([coupling[0], exchanged(coupling[0], 1)])
    my_rows = remap[0, 0]
    other_rows = exchanged(my_rows, 2)

    def padded(plane):
        return jnp.pad(plane.T, ((1, 1), (0, 0)))

    wet_cols, spread_cols = padded(wet), padded(spread)

    def cut(plane, part):
        return lax.dynamic_slice_in_dim(plane, part * width, width + 2, 0)

    pack = jnp.concatenate(
        [
            cut(wet_cols, spot ^ 2),
            cut(spread_cols, spot ^ 2),
            order.reshape(-1, rows),
            jnp.pad(gain, (0, rows - gain.shape[0]))[None],
        ]
    )
    pack = exchanged(pack, 2)
    tall = width + 2
    both_wet = jnp.stack([cut(wet_cols, spot), pack[:tall]])
    both_spread = jnp.stack([cut(spread_cols, spot), pack[tall : 2 * tall]])
    other_order = pack[2 * tall : -1].reshape(order.shape)
    weights = jnp.stack([order.T, other_order.T])
    gains = jnp.stack([gain, pack[-1, : gain.shape[0]]])
    gains = jnp.broadcast_to(gains[:, :, None], gains.shape + (rows,))
    rows_from = jnp.stack([my_rows, other_rows])

    side_columns = [field[:, :, 0], field[:, :, cols - 1]]
    own = jnp.stack([field[:, 0, :], field[:, rows - 1, :]] + side_columns)
    lent = jnp.stack(
        [
            lax.dynamic_index_in_dim(field, other_rows[0], 1, False),
            lax.dynamic_index_in_dim(field, other_rows[rows - 1], 1, False),
        ]
        + side_columns
    )
    own_all = jnp.concatenate([own, exchanged(own, 1)], axis=1)
    pulled = jnp.concatenate([exchanged(lent, 2), exchanged(lent, 3)], axis=1)
    choose = (jnp.arange(rows)[:, None] == my_rows[None, :]).astype(jnp.float32)
    pulled_columns = jnp.einsum("slq,qr->slr", pulled[2:], choose, precision=HIGHEST)
    coupled = own_all + gain[None, :, None] * jnp.concatenate([pulled[:2], pulled_columns])
    solved = jnp.einsum("kl,skx->slx", order[:, :half], coupled, precision=HIGHEST)

    def border(plane):
        return jnp.stack([plane[0], plane[rows - 1], plane[:, 0], plane[:, cols - 1]])[:, None, :]

    halo = tile_halo(solved * border(spread), *near)
    blocks = []
    for part in range(PARTS):
        span = slice(part * width, (part + 1) * width)
        ends = jnp.concatenate([halo[0][:, span], halo[1][:, span]], axis=1)
        ends = jnp.pad(ends, ((0, 0), (0, rows - 2 * width)))
        blocks.append(jnp.stack([halo[2] if part == 0 else halo[3], ends]))
    blocks = jnp.stack(blocks)
    halos = [blocks[spot]] + [exchanged(blocks[spot ^ bits], bits) for bits in range(1, PARTS)]

    results, edges = two_steps(
        place, arrived, weights, gains, rows_from, both_wet, both_spread, halos
    )

    edges = [edges[0]] + [exchanged(edges[bits], bits) for bits in range(1, PARTS)]
    results = [results[0]] + [exchanged(results[bits], bits) for bits in range(1, PARTS)]
    edges = jnp.stack(edges)[spot ^ jnp.arange(PARTS)]
    top = jnp.concatenate([edges[part, 2, :, :width] for part in range(PARTS)], axis=1)
    bottom = jnp.concatenate([edges[part, 2, :, width : 2 * width] for part in range(PARTS)], axis=1)
    halo = tile_halo(jnp.stack([top, bottom, edges[0, 0], edges[PARTS - 1, 1]]), *near)
    sides = []
    for part in range(PARTS):
        left = halo[2] if part == 0 else edges[part - 1, 1]
        right = halo[3] if part == PARTS - 1 else edges[part + 1, 0]
        sides.append(
            jnp.stack([left * wet[:, part * width], right * wet[:, (part + 1) * width - 1]])
        )
    top_bottom = jnp.stack([halo[0] * wet[0], halo[1] * wet[rows - 1]])
    return join_columns(results, place, jnp.stack(sides), top_bottom)[None, None]


def solution(mesh):
    in_specs = (
        P("sect", "tile", "lev", None, None),
        P("sect", "tile", None, None),
        P("sect", "tile", None, None),
        P("sect", "tile", None),
        P("sect", "lev"),
        P("sect", "tile", None, None),
        P("tile", None),
        P("tile", None),
        P("tile", None),
    )
    out_specs = P("sect", "tile", "lev", None, None)
    return jax.shard_map(
        on_device, mesh=mesh, in_specs=in_specs, out_specs=out_specs, check_vma=False
    )
```

```python
import jax
import jax.numpy as jnp
from jax import lax
from jax.experimental import pallas as pl
from jax.experimental.pallas import tpu as pltpu
from jax.sharding import PartitionSpec as P

Z = ("sect", "lev")
PARTS = 4
HIGHEST = lax.Precision.HIGHEST
SMEM = pl.BlockSpec(memory_space=pltpu.SMEM)
VMEM = pl.BlockSpec(memory_space=pltpu.VMEM)


def traded(blocks):
    return lax.all_to_all(blocks, Z, 0, 0)


def exchanged(block, bits):
    return lax.ppermute(block, Z, [(at, at ^ bits) for at in range(PARTS)])


def all_exchanged(blocks):
    return [blocks[0]] + [exchanged(blocks[bits], bits) for bits in range(1, PARTS)]


def split_kernel(place, lent_rows, field, gain, p0, p1, p2, p3, borders, turned):
    levels, rows, cols = field.shape
    width = cols // PARTS
    turned[0] = jnp.zeros((levels, rows), jnp.float32)
    turned[cols + 1] = jnp.zeros((levels, rows), jnp.float32)
    flat = turned.reshape((cols + 2) * levels, rows)
    for level in range(levels):
        flat[pl.ds(levels + level, cols, stride=levels), :] = field[level].T
    for bits, part in enumerate((p0, p1, p2, p3)):
        part[...] = turned[pl.ds((place[0] ^ bits) * width, width + 2)]
    component = place[0] // 2
    for at in range(PARTS):
        lent = component != at // 2
        for slot, fixed in enumerate((0, rows - 1)):
            row = jnp.where(lent, lent_rows[fixed], fixed)
            borders[at, slot * levels : (slot + 1) * levels, :] = field[:, pl.ds(row, 1), :].reshape(levels, cols)
        borders[at, 2 * levels : 3 * levels, :] = turned[1]
        borders[at, 3 * levels : 4 * levels, :] = turned[cols]
        borders[at, 4 * levels :, :] = gain[...]


def split_columns(place, lent_rows, field, gain):
    levels, rows, cols = field.shape
    part = jax.ShapeDtypeStruct((cols // PARTS + 2, levels, rows), jnp.float32)
    *parts, borders = pl.pallas_call(
        split_kernel,
        out_shape=[part] * PARTS + [jax.ShapeDtypeStruct((PARTS, 4 * levels + 1, rows), jnp.float32)],
        in_specs=[SMEM, SMEM, VMEM, VMEM],
        out_specs=[VMEM] * (PARTS + 1),
        scratch_shapes=[pltpu.VMEM((cols + 2, levels, rows), jnp.float32)],
        name="split_columns",
    )(place, lent_rows, field, gain)
    return parts, borders


def join_kernel(place, p0, p1, p2, p3, sides, top_bottom, out, turned):
    levels, rows, cols = out.shape
    width = cols // PARTS
    for bits, part in enumerate((p0, p1, p2, p3)):
        turned[pl.ds((place[0] ^ bits) * width, width)] = part[...]
    for part in range(PARTS):
        for side in range(2):
            at = part * width + side * (width - 1)
            turned[at] = turned[at] + sides[part, side]
    flat = turned.reshape(cols * levels, rows)
    row = lax.broadcasted_iota(jnp.int32, (rows, cols), 0)
    for level in range(levels):
        plane = flat[pl.ds(level, cols, stride=levels), :].T
        top = top_bottom[0, level : level + 1, :]
        bottom = top_bottom[1, level : level + 1, :]
        out[level] = plane + jnp.where(row == 0, top, jnp.where(row == rows - 1, bottom, 0.0))


def join_columns(place, parts, sides, top_bottom):
    width, levels, rows = parts[0].shape
    cols = width * PARTS
    return pl.pallas_call(
        join_kernel,
        out_shape=jax.ShapeDtypeStruct((levels, rows, cols), jnp.float32),
        in_specs=[SMEM] + [VMEM] * 6,
        out_specs=VMEM,
        scratch_shapes=[pltpu.VMEM((cols, levels, rows), jnp.float32)],
        name="join_columns",
    )(place, *parts, sides, top_bottom)


def halves(value):
    high = value.astype(jnp.bfloat16)
    low = (value - high.astype(jnp.float32)).astype(jnp.bfloat16)
    return high, low


def picked(value, index):
    return jnp.take_along_axis(value, index, axis=1, mode="promise_in_bounds")


def steps_kernel(
    place, p0, p1, p2, p3, weights, gains, rows_from, wet, spread, halos,
    o0, o1, o2, o3, edges, column, state,
):
    parts, outs = (p0, p1, p2, p3), (o0, o1, o2, o3)
    wide, half, rows = p0.shape
    spot = place[0]
    component, swap = spot // 2, spot % 2
    comps = [component, 1 - component]
    width = wide - 2
    levels = 2 * half
    at_once, few = 16, 8
    lane = lax.broadcasted_iota(jnp.int32, (levels, rows), 1)
    mixes, picks = [], []
    for comp in range(2):
        mix = weights[comps[comp]]
        turned = jnp.concatenate([mix[half:], mix[:half]], axis=0)
        turned = jnp.concatenate([turned[:, half:], turned[:, :half]], axis=1)
        high, low = halves(jnp.where(swap == 0, mix, turned))
        mixes.append(jnp.concatenate([high, low, high], axis=1))
        picks.append(jnp.broadcast_to(rows_from[pl.ds(comps[comp], 1), :], (levels, rows)))

    def joined(blocks, comp, *at):
        return jnp.concatenate(
            [blocks[(spot ^ (2 * comp + part),) + at] for part in range(2)], axis=0
        )

    gain = [joined(gains, comp) for comp in range(2)]

    def solve(load, first, store, count):
        for comp in range(2):
            rights = []
            for at in range(count):
                coupled = load(comp, first + at)
                coupled = coupled + gain[comp] * picked(load(1 - comp, first + at), picks[comp])
                high, low = halves(coupled)
                rights.append(jnp.concatenate([high, high, low], axis=0))
            for at in range(0, count, 2):
                pair = jnp.concatenate(rights[at : at + 2], axis=1)
                solved = jnp.dot(mixes[comp], pair, preferred_element_type=jnp.float32)
                for side in range(2):
                    column[comp, store + at + side] = solved[:, side * rows : (side + 1) * rows]

    def flux(comp, at):
        return column[comp, at] * spread[comps[comp], pl.ds(at, 1), :]

    def lap(around, ends):
        mid = around[1]
        above = jnp.where(lane == 0, ends, pltpu.roll(mid, 1, 1))
        below = jnp.where(lane == rows - 1, ends, pltpu.roll(mid, rows - 1, 1))
        return above + below + around[0] + around[2] - 4.0 * mid

    def arrived(comp, at):
        return jnp.concatenate([parts[2 * comp][at], parts[2 * comp + 1][at]], axis=0)

    def first_solve(step, carry):
        solve(arrived, step * at_once, step * at_once, at_once)
        return carry

    whole, rest = divmod(wide, at_once)
    lax.fori_loop(0, whole, first_solve, 0)
    if rest:
        solve(arrived, whole * at_once, whole * at_once, rest)
    tops = [joined(halos, comp, 1) for comp in range(2)]
    outer = []
    for comp in range(2):
        across = joined(halos, comp, 0)
        outer.append(
            (
                jnp.where(place[0] == 0, across, flux(comp, 0)),
                jnp.where(place[0] == PARTS - 1, across, flux(comp, width + 1)),
            )
        )

    def spread_first(first, left, right):
        for comp in range(2):
            fluxes = [flux(comp, first + at) for at in range(few + 2)]
            if left:
                fluxes[0] = outer[comp][0]
            if right:
                fluxes[-1] = outer[comp][1]
            for at in range(few):
                j = first + at
                ends = picked(tops[comp], jnp.where(lane == 0, j, j + width))
                total = column[comp, j + 1] + lap(fluxes[at : at + 3], ends)
                state[comp, j] = wet[comps[comp], pl.ds(j + 1, 1), :] * total

    for first in range(0, width, few):
        spread_first(first, first == 0, first + few == width)

    def held(comp, at):
        return state[comp, at]

    def second_solve(step, carry):
        solve(held, step * at_once, step * at_once + 1, at_once)
        return carry

    lax.fori_loop(0, width // at_once, second_solve, 0)
    for comp in range(2):
        column[comp, 0] = jnp.zeros((levels, rows), jnp.float32)
        column[comp, width + 1] = jnp.zeros((levels, rows), jnp.float32)

    def second_spread(step, carry):
        kept = []
        for comp in range(2):
            first = step * few
            fluxes = [flux(comp, first + at) for at in range(few + 2)]
            both = carry[comp]
            for at in range(few):
                j = first + at
                total = column[comp, j + 1] + lap(fluxes[at : at + 3], 0.0)
                done = wet[comps[comp], pl.ds(j + 1, 1), :] * total
                outs[2 * comp][j] = done[:half]
                outs[2 * comp + 1][j] = done[half:]
                ends = picked(fluxes[at + 1], jnp.where(lane == j, 0, rows - 1))
                both = jnp.where((lane == j) | (lane == j + width), ends, both)
            kept.append(both)
        return tuple(kept)

    empty = jnp.zeros((levels, rows), jnp.float32)
    both = lax.fori_loop(0, width // few, second_spread, (empty, empty))
    for comp in range(2):
        for slot, value in enumerate((flux(comp, 1), flux(comp, width), both[comp])):
            edges[spot ^ (2 * comp), slot] = value[:half]
            edges[spot ^ (2 * comp + 1), slot] = value[half:]


def two_steps(place, parts, weights, gains, rows_from, wet, spread, halos):
    wide, half, rows = parts[0].shape
    width = wide - 2
    part = jax.ShapeDtypeStruct((width, half, rows), jnp.float32)
    *results, edges = pl.pallas_call(
        steps_kernel,
        out_shape=[part] * PARTS + [jax.ShapeDtypeStruct((PARTS, 3, half, rows), jnp.float32)],
        in_specs=[SMEM] + [VMEM] * 10,
        out_specs=[VMEM] * (PARTS + 1),
        scratch_shapes=[
            pltpu.VMEM((2, wide, 2 * half, rows), jnp.float32),
            pltpu.VMEM((2, width, 2 * half, rows), jnp.float32),
        ],
        name="two_steps",
    )(place, *parts, weights, gains, rows_from, wet, spread, halos)
    return results, edges


def tile_halo(edges, nbr_tile, nbr_side, nbr_flip):
    every = lax.all_gather(edges, "tile", axis=0)
    found = every[jnp.maximum(nbr_tile, 0), nbr_side]
    turned = jnp.where((nbr_flip == 1)[:, None, None], found[..., ::-1], found)
    return jnp.where((nbr_tile >= 0)[:, None, None], turned, jnp.float32(0.0))


def on_device(
    adjoint, diffusion, wet_mask, remap, coupling, vert_inverse, nbr_tile, nbr_side, nbr_flip
):
    field = adjoint[0, 0]
    half, rows, cols = field.shape
    width = cols // PARTS
    component, level_at = lax.axis_index("sect"), lax.axis_index("lev")
    spot = component * 2 + level_at
    place = spot[None].astype(jnp.int32)
    wet = wet_mask[0, 0].astype(jnp.float32)
    spread = wet * diffusion[0, 0]
    near = (nbr_tile[0], nbr_side[0], nbr_flip[0])
    inverse = vert_inverse[0, 0]
    my_rows = remap[0, 0]

    def both(mine, other):
        return jnp.where(component == 0, jnp.stack([mine, other]), jnp.stack([other, mine]))

    other_rows = exchanged(my_rows, 2)

    def padded(plane):
        return jnp.pad(plane.T, ((1, 1), (0, 0)))

    wet_cols, spread_cols = padded(wet), padded(spread)

    def cut(plane, part):
        return lax.dynamic_slice_in_dim(plane, part * width, width + 2, 0)

    def packed(part):
        return jnp.concatenate([cut(wet_cols, part), cut(spread_cols, part), inverse.reshape(-1, rows)])

    packs = both(packed(spot), exchanged(packed(spot ^ 2), 2))
    tall = width + 2
    both_wet, both_spread = packs[:, :tall], packs[:, tall : 2 * tall]
    weights = packs[:, 2 * tall :].reshape((2,) + inverse.shape).transpose(0, 2, 1)
    rows_from = both(my_rows, other_rows)

    gain = jnp.pad(coupling, ((0, 0), (0, rows - half)))
    parts, borders = split_columns(place, other_rows, field, gain)
    borders = traded(borders)
    parts = all_exchanged(parts)

    gains = borders[:, -1, :half].reshape(2, 2 * half)
    borders = borders[:, :-1].reshape(2, 2, 4, half, rows)
    borders = borders.transpose(0, 2, 1, 3, 4).reshape(2, 4, 2 * half, rows)
    own, pulled = [jnp.where(component == comp, borders[0], borders[1]) for comp in range(2)]
    my_gain = jnp.where(component == 0, gains[0], gains[1])
    choose = (jnp.arange(rows)[:, None] == my_rows[None, :]).astype(jnp.float32)
    pulled_columns = jnp.einsum("slq,qr->slr", pulled[2:], choose, precision=HIGHEST)
    coupled = own + my_gain[None, :, None] * jnp.concatenate([pulled[:2], pulled_columns])
    mine = lax.dynamic_slice_in_dim(inverse, level_at * half, half, 1)
    solved = jnp.einsum("kl,skx->slx", mine, coupled, precision=HIGHEST)

    def border(plane):
        return jnp.stack([plane[0], plane[rows - 1], plane[:, 0], plane[:, cols - 1]])[:, None, :]

    halo = tile_halo(solved * border(spread), *near)
    blocks = []
    for part in range(PARTS):
        span = slice(part * width, (part + 1) * width)
        ends = jnp.concatenate([halo[0][:, span], halo[1][:, span]], axis=1)
        ends = jnp.pad(ends, ((0, 0), (0, rows - 2 * width)))
        blocks.append(jnp.stack([halo[2] if part == 0 else halo[3], ends]))
    halos = traded(jnp.stack(blocks))

    gains = jnp.broadcast_to(gains.reshape(PARTS, half, 1), (PARTS, half, rows))
    results, edges = two_steps(
        place, parts, weights, gains, rows_from, both_wet, both_spread, halos
    )

    edges = traded(edges)
    results = all_exchanged(results)
    top = jnp.concatenate([edges[part, 2, :, :width] for part in range(PARTS)], axis=1)
    bottom = jnp.concatenate([edges[part, 2, :, width : 2 * width] for part in range(PARTS)], axis=1)
    halo = tile_halo(jnp.stack([top, bottom, edges[0, 0], edges[PARTS - 1, 1]]), *near)
    sides = []
    for part in range(PARTS):
        left = halo[2] if part == 0 else edges[part - 1, 1]
        right = halo[3] if part == PARTS - 1 else edges[part + 1, 0]
        sides.append(
            jnp.stack([left * wet[:, part * width], right * wet[:, (part + 1) * width - 1]])
        )
    top_bottom = jnp.stack([halo[0] * wet[0], halo[1] * wet[rows - 1]])
    return join_columns(place, results, jnp.stack(sides), top_bottom)[None, None]


def solution(mesh):
    in_specs = (
        P("sect", "tile", "lev", None, None),
        P("sect", "tile", None, None),
        P("sect", "tile", None, None),
        P("sect", "tile", None),
        P("sect", "lev"),
        P("sect", "tile", None, None),
        P("tile", None),
        P("tile", None),
        P("tile", None),
    )
    out_specs = P("sect", "tile", "lev", None, None)
    return jax.shard_map(
        on_device, mesh=mesh, in_specs=in_specs, out_specs=out_specs, check_vma=False
    )
```

```python
import jax
import jax.numpy as jnp
from jax import lax
from jax.experimental import pallas as pl
from jax.experimental.pallas import tpu as pltpu
from jax.sharding import PartitionSpec as P

Z = ("sect", "lev")
PARTS = 4
BLOCK = 8
FIRST = 16
HIGHEST = lax.Precision.HIGHEST
SMEM = pl.BlockSpec(memory_space=pltpu.SMEM)
VMEM = pl.BlockSpec(memory_space=pltpu.VMEM)


def traded(blocks):
    return lax.all_to_all(blocks, Z, 0, 0)


def exchanged(block, bits):
    return lax.ppermute(block, Z, [(at, at ^ bits) for at in range(PARTS)])


def all_exchanged(blocks):
    return [blocks[0]] + [exchanged(blocks[bits], bits) for bits in range(1, PARTS)]


def pack_kernel(place, mask, diffusion, inverse, remap, mine, sent):
    rows, cols = mask.shape
    levels = inverse.shape[0]
    half, wide = levels // 2, cols // PARTS + 2
    wet = mask[...].astype(jnp.float32)
    nothing = jnp.zeros((1, rows), jnp.float32)
    folded = jnp.concatenate([inverse[:half, :], inverse[half:, :]], axis=1)
    for pack, part in ((mine, place[0]), (sent, place[0] ^ 2)):
        for slot, plane in enumerate((wet.T, (wet * diffusion[...]).T)):
            block = jnp.concatenate([nothing, plane, nothing], axis=0)
            for at in range(PARTS):

                @pl.when(part == at)
                def _():
                    first = at * (wide - 2)
                    pack[slot * wide : (slot + 1) * wide, :] = block[first : first + wide]

        pack[2 * wide : 2 * wide + half, :] = folded
        pack[2 * wide + half :, :] = remap[...].astype(jnp.float32)


def parameters(place, mask, diffusion, inverse, remap):
    rows, cols = mask.shape
    count = 2 * (cols // PARTS + 2) + inverse.shape[0] // 2 + 1
    pack = jax.ShapeDtypeStruct((count, rows), jnp.float32)
    return pl.pallas_call(
        pack_kernel,
        out_shape=[pack, pack],
        in_specs=[SMEM] + [VMEM] * 4,
        out_specs=[VMEM, VMEM],
        name="parameters",
    )(place, mask, diffusion, inverse, remap)


def split_kernel(place, field, p0, p1, p2, p3, q2, ends, turned):
    levels, rows, cols = field.shape
    width = cols // PARTS
    turned[0] = jnp.zeros((levels, rows), jnp.float32)
    turned[cols + 1] = jnp.zeros((levels, rows), jnp.float32)
    flat = turned.reshape((cols + 2) * levels, rows)
    for level in range(levels):
        flat[pl.ds(levels + level, cols, stride=levels), :] = field[level].T
    for bits, part in ((0, p0), (1, p1), (2, p2), (3, p3)):
        part[...] = turned[pl.ds((place[0] ^ bits) * width, part.shape[0])]
    q2[...] = turned[pl.ds((place[0] ^ 2) * width + p2.shape[0], q2.shape[0])]
    ends[0] = turned[1]
    ends[1] = turned[cols]


def split_columns(place, field):
    levels, rows, cols = field.shape
    wide = cols // PARTS + 2
    counts = [wide, wide, FIRST, wide, wide - FIRST, 2]
    return pl.pallas_call(
        split_kernel,
        grid=(levels // BLOCK,),
        out_shape=[jax.ShapeDtypeStruct((count, levels, rows), jnp.float32) for count in counts],
        in_specs=[SMEM, pl.BlockSpec((BLOCK, rows, cols), lambda i: (i, 0, 0))],
        out_specs=[pl.BlockSpec((count, BLOCK, rows), lambda i: (0, i, 0)) for count in counts],
        scratch_shapes=[pltpu.VMEM((cols + 2, BLOCK, rows), jnp.float32)],
        name="split_columns",
    )(place, field)


def border_kernel(place, lent_rows, field, ends, gain, borders, held, arrivals):
    levels, rows, cols = field.shape
    wanted = (0, rows - 1, lent_rows[0], lent_rows[rows - 1])
    copies = [
        pltpu.make_async_copy(field.at[:, pl.ds(row, 1), :], held.at[slot], arrivals.at[slot])
        for slot, row in enumerate(wanted)
    ]
    for copy in copies:
        copy.start()
    for copy in copies:
        copy.wait()
    component = place[0] // 2
    for at in range(PARTS):
        lent = (component != at // 2).astype(jnp.int32)
        for slot in range(2):
            borders[at, slot * levels : (slot + 1) * levels, :] = held[2 * lent + slot].reshape(levels, cols)
            borders[at, (2 + slot) * levels : (3 + slot) * levels, :] = ends[slot]
        borders[at, 4 * levels :, :] = jnp.zeros((1, rows), jnp.float32)
        borders[at, 4 * levels :, :levels] = gain[...]


def side_borders(place, lent_rows, field, ends, gain):
    levels, rows, cols = field.shape
    return pl.pallas_call(
        border_kernel,
        out_shape=jax.ShapeDtypeStruct((PARTS, 4 * levels + 1, rows), jnp.float32),
        in_specs=[SMEM, SMEM, pl.BlockSpec(memory_space=pl.ANY), VMEM, VMEM],
        out_specs=VMEM,
        scratch_shapes=[pltpu.VMEM((4, levels, 1, cols), jnp.float32), pltpu.SemaphoreType.DMA((4,))],
        name="side_borders",
    )(place, lent_rows, field, ends, gain)


def join_kernel(place, p0, p1, p2, p3, sides, top_bottom, out, turned):
    levels, rows, cols = out.shape
    width = cols // PARTS
    for bits, part in enumerate((p0, p1, p2, p3)):
        turned[pl.ds((place[0] ^ bits) * width, width)] = part[...]
    for part in range(PARTS):
        for side in range(2):
            at = part * width + side * (width - 1)
            turned[at] = turned[at] + sides[part, side]
    flat = turned.reshape(cols * levels, rows)
    row = lax.broadcasted_iota(jnp.int32, (rows, cols), 0)
    for level in range(levels):
        plane = flat[pl.ds(level, cols, stride=levels), :].T
        top = top_bottom[0, level : level + 1, :]
        bottom = top_bottom[1, level : level + 1, :]
        out[level] = plane + jnp.where(row == 0, top, jnp.where(row == rows - 1, bottom, 0.0))


def join_columns(place, parts, sides, top_bottom):
    width, levels, rows = parts[0].shape
    cols = width * PARTS
    return pl.pallas_call(
        join_kernel,
        grid=(levels // BLOCK,),
        out_shape=jax.ShapeDtypeStruct((levels, rows, cols), jnp.float32),
        in_specs=[SMEM]
        + [pl.BlockSpec((width, BLOCK, rows), lambda i: (0, i, 0))] * PARTS
        + [
            pl.BlockSpec((PARTS, 2, BLOCK, rows), lambda i: (0, 0, i, 0)),
            pl.BlockSpec((2, BLOCK, cols), lambda i: (0, i, 0)),
        ],
        out_specs=pl.BlockSpec((BLOCK, rows, cols), lambda i: (i, 0, 0)),
        scratch_shapes=[pltpu.VMEM((cols, BLOCK, rows), jnp.float32)],
        name="join_columns",
    )(place, *parts, sides, top_bottom)


def halves(value):
    high = value.astype(jnp.bfloat16)
    low = (value - high.astype(jnp.float32)).astype(jnp.bfloat16)
    return high, low


def picked(value, index):
    return jnp.take_along_axis(value, index, axis=1, mode="promise_in_bounds")


def steps_kernel(
    place, p0, p1, p2, p3, q2, my_pack, other_pack, gains, halos,
    o0, o1, o2, o3, edges, column, state,
):
    outs = (o0, o1, o2, o3)
    wide, half, rows = p0.shape
    spot, width = place[0], wide - 2
    packs = (my_pack, other_pack)
    at_once, few = 16, 8
    levels = 2 * half
    lane = lax.broadcasted_iota(jnp.int32, (levels, rows), 1)
    mixes, picks = [], []
    for pack in packs:
        folded = pack[2 * wide : 2 * wide + half, :].T
        mix = jnp.concatenate([folded[:levels], folded[levels:]], axis=1)
        turned = jnp.concatenate([mix[half:], mix[:half]], axis=0)
        turned = jnp.concatenate([turned[:, half:], turned[:, :half]], axis=1)
        high, low = halves(jnp.where(spot % 2 == 0, mix, turned))
        mixes.append(jnp.concatenate([high, low, high], axis=1))
        pick = pack[2 * wide + half :, :].astype(jnp.int32)
        picks.append(jnp.broadcast_to(pick, (levels, rows)))

    def joined(blocks, comp, *at):
        return jnp.concatenate(
            [blocks[(spot ^ (2 * comp + part),) + at] for part in range(2)], axis=0
        )

    gain = []
    for comp in range(2):
        parts_of = [jnp.broadcast_to(gains[spot ^ (2 * comp + part)], (rows, rows)).T for part in range(2)]
        gain.append(jnp.concatenate([block[:half] for block in parts_of], axis=0))

    def solve(load, first, store, count):
        for comp in range(2):
            rights = []
            for at in range(count):
                coupled = load(comp, first + at)
                coupled = coupled + gain[comp] * picked(load(1 - comp, first + at), picks[comp])
                high, low = halves(coupled)
                rights.append(jnp.concatenate([high, high, low], axis=0))
            for at in range(0, count, 2):
                pair = jnp.concatenate(rights[at : at + 2], axis=1)
                solved = jnp.dot(mixes[comp], pair, preferred_element_type=jnp.float32)
                for side in range(2):
                    column[comp, store + at + side] = solved[:, side * rows : (side + 1) * rows]

    def flux(comp, at):
        return column[comp, at] * packs[comp][pl.ds(wide + at, 1), :]

    def lap(around, ends):
        mid = around[1]
        above = jnp.where(lane == 0, ends, pltpu.roll(mid, 1, 1))
        below = jnp.where(lane == rows - 1, ends, pltpu.roll(mid, rows - 1, 1))
        return above + below + around[0] + around[2] - 4.0 * mid

    def arrived(comp, at):
        if comp == 0:
            blocks = [p0[at], p1[at]]
        else:
            blocks = [p2[at] if at < FIRST else q2[at - FIRST], p3[at]]
        return jnp.concatenate(blocks, axis=0)

    for first in range(0, wide, at_once):
        solve(arrived, first, first, min(at_once, wide - first))
    tops = [joined(halos, comp, 1) for comp in range(2)]
    outer = []
    for comp in range(2):
        across = joined(halos, comp, 0)
        outer.append(
            (
                jnp.where(place[0] == 0, across, flux(comp, 0)),
                jnp.where(place[0] == PARTS - 1, across, flux(comp, width + 1)),
            )
        )

    def spread_first(first, left, right):
        for comp in range(2):
            fluxes = [flux(comp, first + at) for at in range(few + 2)]
            if left:
                fluxes[0] = outer[comp][0]
            if right:
                fluxes[-1] = outer[comp][1]
            for at in range(few):
                j = first + at
                ends = picked(tops[comp], jnp.where(lane == 0, j, j + width))
                total = column[comp, j + 1] + lap(fluxes[at : at + 3], ends)
                state[comp, j] = packs[comp][pl.ds(j + 1, 1), :] * total

    for first in range(0, width, few):
        spread_first(first, first == 0, first + few == width)

    def held(comp, at):
        return state[comp, at]

    def second_solve(step, carry):
        solve(held, step * at_once, step * at_once + 1, at_once)
        return carry

    lax.fori_loop(0, width // at_once, second_solve, 0)
    for comp in range(2):
        column[comp, 0] = jnp.zeros((levels, rows), jnp.float32)
        column[comp, width + 1] = jnp.zeros((levels, rows), jnp.float32)

    def second_spread(step, carry):
        kept = []
        for comp in range(2):
            first = step * few
            fluxes = [flux(comp, first + at) for at in range(few + 2)]
            both = carry[comp]
            for at in range(few):
                j = first + at
                total = column[comp, j + 1] + lap(fluxes[at : at + 3], 0.0)
                done = packs[comp][pl.ds(j + 1, 1), :] * total
                outs[2 * comp][j] = done[:half]
                outs[2 * comp + 1][j] = done[half:]
                ends = picked(fluxes[at + 1], jnp.where(lane == j, 0, rows - 1))
                both = jnp.where((lane == j) | (lane == j + width), ends, both)
            kept.append(both)
        return tuple(kept)

    empty = jnp.zeros((levels, rows), jnp.float32)
    both = lax.fori_loop(0, width // few, second_spread, (empty, empty))
    for comp in range(2):
        for slot, value in enumerate((flux(comp, 1), flux(comp, width), both[comp])):
            edges[spot ^ (2 * comp), slot] = value[:half]
            edges[spot ^ (2 * comp + 1), slot] = value[half:]


def two_steps(place, parts, packs, gains, halos):
    wide, half, rows = parts[0].shape
    width = wide - 2
    part = jax.ShapeDtypeStruct((width, half, rows), jnp.float32)
    *results, edges = pl.pallas_call(
        steps_kernel,
        out_shape=[part] * PARTS + [jax.ShapeDtypeStruct((PARTS, 3, half, rows), jnp.float32)],
        in_specs=[SMEM] + [VMEM] * 9,
        out_specs=[VMEM] * (PARTS + 1),
        scratch_shapes=[
            pltpu.VMEM((2, wide, 2 * half, rows), jnp.float32),
            pltpu.VMEM((2, width, 2 * half, rows), jnp.float32),
        ],
        name="two_steps",
    )(place, *parts, *packs, gains, halos)
    return results, edges


def tile_halo(edges, nbr_tile, nbr_side, nbr_flip):
    every = lax.all_gather(edges, "tile", axis=0)
    found = every[jnp.maximum(nbr_tile, 0), nbr_side]
    turned = jnp.where((nbr_flip == 1)[:, None, None], found[..., ::-1], found)
    return jnp.where((nbr_tile >= 0)[:, None, None], turned, jnp.float32(0.0))


def on_device(
    adjoint, diffusion, wet_mask, remap, coupling, vert_inverse, nbr_tile, nbr_side, nbr_flip
):
    field = adjoint[0, 0]
    half, rows, cols = field.shape
    width = cols // PARTS
    component, level_at = lax.axis_index("sect"), lax.axis_index("lev")
    spot = component * 2 + level_at
    place = spot[None].astype(jnp.int32)
    near = (nbr_tile[0], nbr_side[0], nbr_flip[0])
    inverse = vert_inverse[0, 0]
    my_rows = remap[0, 0]

    own_pack, sent = parameters(place, wet_mask[0, 0], diffusion[0, 0], inverse, remap[0])
    packs = [own_pack, exchanged(sent, 2)]
    other_rows = packs[1][-1].astype(jnp.int32)

    mine, beside, ahead, far, rest, ends = split_columns(place, field)
    ahead = exchanged(ahead, 2)
    borders = side_borders(place, other_rows, field, ends, coupling)
    beside, far, rest, borders, wet_mask, diffusion, inverse = lax.optimization_barrier(
        (beside, far, rest, borders, wet_mask, diffusion, inverse)
    )
    borders = traded(borders)
    parts = [mine, exchanged(beside, 1), ahead, exchanged(far, 3), exchanged(rest, 2)]

    wet = wet_mask[0, 0].astype(jnp.float32)
    spread = wet * diffusion[0, 0]

    gain_rows = borders[:, -1:]
    gains = borders[:, -1, :half].reshape(2, 2 * half)
    borders = borders[:, :-1].reshape(2, 2, 4, half, rows)
    borders = borders.transpose(0, 2, 1, 3, 4).reshape(2, 4, 2 * half, rows)
    own, pulled = [jnp.where(component == comp, borders[0], borders[1]) for comp in range(2)]
    my_gain = jnp.where(component == 0, gains[0], gains[1])
    choose = (jnp.arange(rows)[:, None] == my_rows[None, :]).astype(jnp.float32)
    pulled_columns = jnp.einsum("slq,qr->slr", pulled[2:], choose, precision=HIGHEST)
    coupled = own + my_gain[None, :, None] * jnp.concatenate([pulled[:2], pulled_columns])
    mine = lax.dynamic_slice_in_dim(inverse, level_at * half, half, 1)
    solved = jnp.einsum("kl,skx->slx", mine, coupled, precision=HIGHEST)

    def border(plane):
        return jnp.stack([plane[0], plane[rows - 1], plane[:, 0], plane[:, cols - 1]])[:, None, :]

    halo = tile_halo(solved * border(spread), *near)
    blocks = []
    for part in range(PARTS):
        span = slice(part * width, (part + 1) * width)
        ends = jnp.concatenate([halo[0][:, span], halo[1][:, span]], axis=1)
        ends = jnp.pad(ends, ((0, 0), (0, rows - 2 * width)))
        blocks.append(jnp.stack([halo[2] if part == 0 else halo[3], ends]))
    halos = traded(jnp.stack(blocks))

    results, edges = two_steps(place, parts, packs, gain_rows, halos)

    edges = traded(edges)
    results = all_exchanged(results)
    top = jnp.concatenate([edges[part, 2, :, :width] for part in range(PARTS)], axis=1)
    bottom = jnp.concatenate([edges[part, 2, :, width : 2 * width] for part in range(PARTS)], axis=1)
    halo = tile_halo(jnp.stack([top, bottom, edges[0, 0], edges[PARTS - 1, 1]]), *near)
    sides = []
    for part in range(PARTS):
        left = halo[2] if part == 0 else edges[part - 1, 1]
        right = halo[3] if part == PARTS - 1 else edges[part + 1, 0]
        sides.append(
            jnp.stack([left * wet[:, part * width], right * wet[:, (part + 1) * width - 1]])
        )
    top_bottom = jnp.stack([halo[0] * wet[0], halo[1] * wet[rows - 1]])
    return join_columns(place, results, jnp.stack(sides), top_bottom)[None, None]


def solution(mesh):
    in_specs = (
        P("sect", "tile", "lev", None, None),
        P("sect", "tile", None, None),
        P("sect", "tile", None, None),
        P("sect", "tile", None),
        P("sect", "lev"),
        P("sect", "tile", None, None),
        P("tile", None),
        P("tile", None),
        P("tile", None),
    )
    out_specs = P("sect", "tile", "lev", None, None)
    return jax.shard_map(
        on_device, mesh=mesh, in_specs=in_specs, out_specs=out_specs, check_vma=False
    )
```

```python
import jax
import jax.numpy as jnp
from jax import lax
from jax.experimental import pallas as pl
from jax.experimental.pallas import tpu as pltpu
from jax.sharding import PartitionSpec as P

Z = ("sect", "lev")
PARTS = 4
BLOCK = 16
FIRST = 16
HIGHEST = lax.Precision.HIGHEST
SMEM = pl.BlockSpec(memory_space=pltpu.SMEM)
VMEM = pl.BlockSpec(memory_space=pltpu.VMEM)


def traded(blocks):
    return lax.all_to_all(blocks, Z, 0, 0)


def exchanged(block, bits):
    return lax.ppermute(block, Z, [(at, at ^ bits) for at in range(PARTS)])


def all_exchanged(blocks):
    return [blocks[0]] + [exchanged(blocks[bits], bits) for bits in range(1, PARTS)]


def pack_kernel(place, mask, diffusion, inverse, remap, mine, sent):
    rows, cols = mask.shape
    levels = inverse.shape[0]
    half, wide = levels // 2, cols // PARTS + 2
    wet = mask[...].astype(jnp.float32)
    nothing = jnp.zeros((1, rows), jnp.float32)
    folded = jnp.concatenate([inverse[:half, :], inverse[half:, :]], axis=1)
    for pack, part in ((mine, place[0]), (sent, place[0] ^ 2)):
        for slot, plane in enumerate((wet.T, (wet * diffusion[...]).T)):
            block = jnp.concatenate([nothing, plane, nothing], axis=0)
            for at in range(PARTS):

                @pl.when(part == at)
                def _():
                    first = at * (wide - 2)
                    pack[slot * wide : (slot + 1) * wide, :] = block[first : first + wide]

        pack[2 * wide : 2 * wide + half, :] = folded
        pack[2 * wide + half :, :] = remap[...].astype(jnp.float32)


def parameters(place, mask, diffusion, inverse, remap):
    rows, cols = mask.shape
    count = 2 * (cols // PARTS + 2) + inverse.shape[0] // 2 + 1
    pack = jax.ShapeDtypeStruct((count, rows), jnp.float32)
    return pl.pallas_call(
        pack_kernel,
        out_shape=[pack, pack],
        in_specs=[SMEM] + [VMEM] * 4,
        out_specs=[VMEM, VMEM],
        name="parameters",
    )(place, mask, diffusion, inverse, remap)


def split_kernel(place, field, p0, p1, p2, p3, q2, ends, turned):
    levels, rows, cols = field.shape
    width = cols // PARTS
    turned[0] = jnp.zeros((levels, rows), jnp.float32)
    turned[cols + 1] = jnp.zeros((levels, rows), jnp.float32)
    flat = turned.reshape((cols + 2) * levels, rows)
    for level in range(levels):
        flat[pl.ds(levels + level, cols, stride=levels), :] = field[level].T
    for bits, part in ((0, p0), (1, p1), (2, p2), (3, p3)):
        part[...] = turned[pl.ds((place[0] ^ bits) * width, part.shape[0])]
    q2[...] = turned[pl.ds((place[0] ^ 2) * width + p2.shape[0], q2.shape[0])]
    ends[0] = turned[1]
    ends[1] = turned[cols]


def split_columns(place, field):
    levels, rows, cols = field.shape
    wide = cols // PARTS + 2
    counts = [wide, wide, FIRST, wide, wide - FIRST, 2]
    return pl.pallas_call(
        split_kernel,
        grid=(levels // BLOCK,),
        out_shape=[jax.ShapeDtypeStruct((count, levels, rows), jnp.float32) for count in counts],
        in_specs=[SMEM, pl.BlockSpec((BLOCK, rows, cols), lambda i: (i, 0, 0))],
        out_specs=[pl.BlockSpec((count, BLOCK, rows), lambda i: (0, i, 0)) for count in counts],
        scratch_shapes=[pltpu.VMEM((cols + 2, BLOCK, rows), jnp.float32)],
        name="split_columns",
    )(place, field)


def border_kernel(place, lent_rows, field, ends, gain, borders, held, arrivals):
    levels, rows, cols = field.shape
    wanted = (0, rows - 1, lent_rows[0], lent_rows[rows - 1])
    copies = [
        pltpu.make_async_copy(field.at[:, pl.ds(row, 1), :], held.at[slot], arrivals.at[slot])
        for slot, row in enumerate(wanted)
    ]
    for copy in copies:
        copy.start()
    for copy in copies:
        copy.wait()
    component = place[0] // 2
    for at in range(PARTS):
        lent = (component != at // 2).astype(jnp.int32)
        for slot in range(2):
            borders[at, slot * levels : (slot + 1) * levels, :] = held[2 * lent + slot].reshape(levels, cols)
            borders[at, (2 + slot) * levels : (3 + slot) * levels, :] = ends[slot]
        borders[at, 4 * levels :, :] = jnp.zeros((1, rows), jnp.float32)
        borders[at, 4 * levels :, :levels] = gain[...]


def side_borders(place, lent_rows, field, ends, gain):
    levels, rows, cols = field.shape
    return pl.pallas_call(
        border_kernel,
        out_shape=jax.ShapeDtypeStruct((PARTS, 4 * levels + 1, rows), jnp.float32),
        in_specs=[SMEM, SMEM, pl.BlockSpec(memory_space=pl.ANY), VMEM, VMEM],
        out_specs=VMEM,
        scratch_shapes=[pltpu.VMEM((4, levels, 1, cols), jnp.float32), pltpu.SemaphoreType.DMA((4,))],
        name="side_borders",
    )(place, lent_rows, field, ends, gain)


def join_kernel(place, p0, p1, p2, p3, sides, top_bottom, out, turned):
    levels, rows, cols = out.shape
    width = cols // PARTS
    for bits, part in enumerate((p0, p1, p2, p3)):
        turned[pl.ds((place[0] ^ bits) * width, width)] = part[...]
    for part in range(PARTS):
        for side in range(2):
            at = part * width + side * (width - 1)
            turned[at] = turned[at] + sides[part, side]
    flat = turned.reshape(cols * levels, rows)
    row = lax.broadcasted_iota(jnp.int32, (rows, cols), 0)
    for level in range(levels):
        plane = flat[pl.ds(level, cols, stride=levels), :].T
        top = top_bottom[0, level : level + 1, :]
        bottom = top_bottom[1, level : level + 1, :]
        out[level] = plane + jnp.where(row == 0, top, jnp.where(row == rows - 1, bottom, 0.0))


def join_columns(place, parts, sides, top_bottom):
    width, levels, rows = parts[0].shape
    cols = width * PARTS
    return pl.pallas_call(
        join_kernel,
        grid=(levels // BLOCK,),
        out_shape=jax.ShapeDtypeStruct((levels, rows, cols), jnp.float32),
        in_specs=[SMEM]
        + [pl.BlockSpec((width, BLOCK, rows), lambda i: (0, i, 0))] * PARTS
        + [
            pl.BlockSpec((PARTS, 2, BLOCK, rows), lambda i: (0, 0, i, 0)),
            pl.BlockSpec((2, BLOCK, cols), lambda i: (0, i, 0)),
        ],
        out_specs=pl.BlockSpec((BLOCK, rows, cols), lambda i: (i, 0, 0)),
        scratch_shapes=[pltpu.VMEM((cols, BLOCK, rows), jnp.float32)],
        name="join_columns",
    )(place, *parts, sides, top_bottom)


def halves(value):
    high = value.astype(jnp.bfloat16)
    low = (value - high.astype(jnp.float32)).astype(jnp.bfloat16)
    return high, low


def picked(value, index):
    return jnp.take_along_axis(value, index, axis=1, mode="promise_in_bounds")


def steps_kernel(
    place, p0, p1, p2, p3, q2, my_pack, other_pack, gains, halos,
    o0, o1, o2, o3, edges, column, state,
):
    outs = (o0, o1, o2, o3)
    wide, half, rows = p0.shape
    spot, width = place[0], wide - 2
    packs = (my_pack, other_pack)
    at_once, few = 16, 8
    levels = 2 * half
    lane = lax.broadcasted_iota(jnp.int32, (levels, rows), 1)
    mixes, picks = [], []
    for pack in packs:
        folded = pack[2 * wide : 2 * wide + half, :].T
        mix = jnp.concatenate([folded[:levels], folded[levels:]], axis=1)
        turned = jnp.concatenate([mix[half:], mix[:half]], axis=0)
        turned = jnp.concatenate([turned[:, half:], turned[:, :half]], axis=1)
        high, low = halves(jnp.where(spot % 2 == 0, mix, turned))
        mixes.append(jnp.concatenate([high, low, high], axis=1))
        pick = pack[2 * wide + half :, :].astype(jnp.int32)
        picks.append(jnp.broadcast_to(pick, (levels, rows)))

    def joined(blocks, comp, *at):
        return jnp.concatenate(
            [blocks[(spot ^ (2 * comp + part),) + at] for part in range(2)], axis=0
        )

    gain = []
    for comp in range(2):
        parts_of = [jnp.broadcast_to(gains[spot ^ (2 * comp + part)], (rows, rows)).T for part in range(2)]
        gain.append(jnp.concatenate([block[:half] for block in parts_of], axis=0))

    def solve(load, first, store, count):
        for comp in range(2):
            rights = []
            for at in range(count):
                coupled = load(comp, first + at)
                coupled = coupled + gain[comp] * picked(load(1 - comp, first + at), picks[comp])
                high, low = halves(coupled)
                rights.append(jnp.concatenate([high, high, low], axis=0))
            for at in range(0, count, 2):
                pair = jnp.concatenate(rights[at : at + 2], axis=1)
                solved = jnp.dot(mixes[comp], pair, preferred_element_type=jnp.float32)
                for side in range(2):
                    column[comp, store + at + side] = solved[:, side * rows : (side + 1) * rows]

    def flux(comp, at):
        return column[comp, at] * packs[comp][pl.ds(wide + at, 1), :]

    def lap(around, ends):
        mid = around[1]
        above = jnp.where(lane == 0, ends, pltpu.roll(mid, 1, 1))
        below = jnp.where(lane == rows - 1, ends, pltpu.roll(mid, rows - 1, 1))
        return above + below + around[0] + around[2] - 4.0 * mid

    def arrived(comp, at):
        if comp == 0:
            blocks = [p0[at], p1[at]]
        else:
            blocks = [p2[at] if at < FIRST else q2[at - FIRST], p3[at]]
        return jnp.concatenate(blocks, axis=0)

    for first in range(0, wide, at_once):
        solve(arrived, first, first, min(at_once, wide - first))
    tops = []
    for comp in range(2):
        folded = [halos[spot ^ (2 * comp + part), half:] for part in range(2)]
        folded = [block[:, first : first + 2 * width] for block in folded for first in (0, 2 * width)]
        ends = jnp.concatenate(folded, axis=0)
        tops.append(jnp.concatenate([ends, ends], axis=1))
    outer = []
    for comp in range(2):
        across = joined(halos, comp, slice(0, half))
        outer.append(
            (
                jnp.where(place[0] == 0, across, flux(comp, 0)),
                jnp.where(place[0] == PARTS - 1, across, flux(comp, width + 1)),
            )
        )

    def spread_first(first, left, right):
        for comp in range(2):
            fluxes = [flux(comp, first + at) for at in range(few + 2)]
            if left:
                fluxes[0] = outer[comp][0]
            if right:
                fluxes[-1] = outer[comp][1]
            for at in range(few):
                j = first + at
                ends = picked(tops[comp], jnp.where(lane == 0, j, j + width))
                total = column[comp, j + 1] + lap(fluxes[at : at + 3], ends)
                state[comp, j] = packs[comp][pl.ds(j + 1, 1), :] * total

    for first in range(0, width, few):
        spread_first(first, first == 0, first + few == width)

    def held(comp, at):
        return state[comp, at]

    def second_solve(step, carry):
        solve(held, step * at_once, step * at_once + 1, at_once)
        return carry

    lax.fori_loop(0, width // at_once, second_solve, 0)
    for comp in range(2):
        column[comp, 0] = jnp.zeros((levels, rows), jnp.float32)
        column[comp, width + 1] = jnp.zeros((levels, rows), jnp.float32)

    def second_spread(step, carry):
        kept = []
        for comp in range(2):
            first = step * few
            fluxes = [flux(comp, first + at) for at in range(few + 2)]
            both = carry[comp]
            for at in range(few):
                j = first + at
                total = column[comp, j + 1] + lap(fluxes[at : at + 3], 0.0)
                done = packs[comp][pl.ds(j + 1, 1), :] * total
                outs[2 * comp][j] = done[:half]
                outs[2 * comp + 1][j] = done[half:]
                ends = picked(fluxes[at + 1], jnp.where(lane == j, 0, rows - 1))
                both = jnp.where((lane == j) | (lane == j + width), ends, both)
            kept.append(both)
        return tuple(kept)

    empty = jnp.zeros((levels, rows), jnp.float32)
    both = lax.fori_loop(0, width // few, second_spread, (empty, empty))
    for comp in range(2):
        for part in range(2):
            to, span = spot ^ (2 * comp + part), slice(part * half, (part + 1) * half)
            edges[to, :half] = flux(comp, 1)[span]
            edges[to, half : 2 * half] = flux(comp, width)[span]
            ends = both[comp][span, : 2 * width]
            edges[to, 2 * half :] = jnp.concatenate([ends[: half // 2], ends[half // 2 :]], axis=1)


def two_steps(place, parts, packs, gains, halos):
    wide, half, rows = parts[0].shape
    width = wide - 2
    part = jax.ShapeDtypeStruct((width, half, rows), jnp.float32)
    *results, edges = pl.pallas_call(
        steps_kernel,
        out_shape=[part] * PARTS + [jax.ShapeDtypeStruct((PARTS, 2 * half + half // 2, rows), jnp.float32)],
        in_specs=[SMEM] + [VMEM] * 9,
        out_specs=[VMEM] * (PARTS + 1),
        scratch_shapes=[
            pltpu.VMEM((2, wide, 2 * half, rows), jnp.float32),
            pltpu.VMEM((2, width, 2 * half, rows), jnp.float32),
        ],
        name="two_steps",
    )(place, *parts, *packs, gains, halos)
    return results, edges


def tile_halo(edges, nbr_tile, nbr_side, nbr_flip):
    every = lax.all_gather(edges, "tile", axis=0)
    found = every[jnp.maximum(nbr_tile, 0), nbr_side]
    turned = jnp.where((nbr_flip == 1)[:, None, None], found[..., ::-1], found)
    return jnp.where((nbr_tile >= 0)[:, None, None], turned, jnp.float32(0.0))


def on_device(
    adjoint, diffusion, wet_mask, remap, coupling, vert_inverse, nbr_tile, nbr_side, nbr_flip
):
    field = adjoint[0, 0]
    half, rows, cols = field.shape
    width = cols // PARTS
    component, level_at = lax.axis_index("sect"), lax.axis_index("lev")
    spot = component * 2 + level_at
    place = spot[None].astype(jnp.int32)
    near = (nbr_tile[0], nbr_side[0], nbr_flip[0])
    inverse = vert_inverse[0, 0]
    my_rows = remap[0, 0]

    own_pack, sent = parameters(place, wet_mask[0, 0], diffusion[0, 0], inverse, remap[0])
    packs = [own_pack, exchanged(sent, 2)]
    other_rows = packs[1][-1].astype(jnp.int32)

    mine, beside, ahead, far, rest, ends = split_columns(place, field)
    ahead = exchanged(ahead, 2)
    borders = side_borders(place, other_rows, field, ends, coupling)
    beside, far, rest, borders, wet_mask, diffusion, inverse = lax.optimization_barrier(
        (beside, far, rest, borders, wet_mask, diffusion, inverse)
    )
    borders = traded(borders)
    parts = [mine, exchanged(beside, 1), ahead, exchanged(far, 3), exchanged(rest, 2)]

    wet = wet_mask[0, 0].astype(jnp.float32)
    spread = wet * diffusion[0, 0]

    gain_rows = borders[:, -1:]
    gains = borders[:, -1, :half].reshape(2, 2 * half)
    borders = borders[:, :-1].reshape(2, 2, 4, half, rows)
    borders = borders.transpose(0, 2, 1, 3, 4).reshape(2, 4, 2 * half, rows)
    own, pulled = [jnp.where(component == comp, borders[0], borders[1]) for comp in range(2)]
    my_gain = jnp.where(component == 0, gains[0], gains[1])
    choose = (jnp.arange(rows)[:, None] == my_rows[None, :]).astype(jnp.float32)
    pulled_columns = jnp.einsum("slq,qr->slr", pulled[2:], choose, precision=HIGHEST)
    coupled = own + my_gain[None, :, None] * jnp.concatenate([pulled[:2], pulled_columns])
    mine = lax.dynamic_slice_in_dim(inverse, level_at * half, half, 1)
    solved = jnp.einsum("kl,skx->slx", mine, coupled, precision=HIGHEST)

    def border(plane):
        return jnp.stack([plane[0], plane[rows - 1], plane[:, 0], plane[:, cols - 1]])[:, None, :]

    halo = tile_halo(solved * border(spread), *near)
    blocks = []
    for part in range(PARTS):
        span = slice(part * width, (part + 1) * width)
        ends = jnp.concatenate([halo[0][:, span], halo[1][:, span]], axis=1)
        ends = jnp.concatenate([ends[: half // 2], ends[half // 2 :]], axis=1)
        blocks.append(jnp.concatenate([halo[2] if part == 0 else halo[3], ends]))
    halos = traded(jnp.stack(blocks))

    results, edges = two_steps(place, parts, packs, gain_rows, halos)

    edges = traded(edges)
    results = all_exchanged(results)
    starts, stops, folded = edges[:, :half], edges[:, half : 2 * half], edges[:, 2 * half :]
    folded = folded.reshape(PARTS, half // 2, 2, 2, width).transpose(3, 2, 1, 0, 4).reshape(2, half, cols)
    halo = tile_halo(jnp.concatenate([folded, starts[:1], stops[PARTS - 1 :]]), *near)
    sides = []
    for part in range(PARTS):
        left = halo[2] if part == 0 else stops[part - 1]
        right = halo[3] if part == PARTS - 1 else starts[part + 1]
        sides.append(
            jnp.stack([left * wet[:, part * width], right * wet[:, (part + 1) * width - 1]])
        )
    top_bottom = jnp.stack([halo[0] * wet[0], halo[1] * wet[rows - 1]])
    return join_columns(place, results, jnp.stack(sides), top_bottom)[None, None]


def solution(mesh):
    in_specs = (
        P("sect", "tile", "lev", None, None),
        P("sect", "tile", None, None),
        P("sect", "tile", None, None),
        P("sect", "tile", None),
        P("sect", "lev"),
        P("sect", "tile", None, None),
        P("tile", None),
        P("tile", None),
        P("tile", None),
    )
    out_specs = P("sect", "tile", "lev", None, None)
    return jax.shard_map(
        on_device, mesh=mesh, in_specs=in_specs, out_specs=out_specs, check_vma=False
    )
```

```python
import jax
import jax.numpy as jnp
from jax import lax
from jax.experimental import pallas as pl
from jax.experimental.pallas import tpu as pltpu
from jax.sharding import PartitionSpec as P

Z = ("sect", "lev")
PARTS = 4
BLOCK = 16
FIRST = 16
HIGHEST = lax.Precision.HIGHEST
SMEM = pl.BlockSpec(memory_space=pltpu.SMEM)
VMEM = pl.BlockSpec(memory_space=pltpu.VMEM)


def in_vmem(block):
    return pltpu.with_memory_space_constraint(block, pltpu.VMEM)


def traded(blocks):
    return lax.all_to_all(blocks, Z, 0, 0)


def exchanged(block, bits):
    return lax.ppermute(block, Z, [(at, at ^ bits) for at in range(PARTS)])


def all_exchanged(blocks):
    return [blocks[0]] + [exchanged(blocks[bits], bits) for bits in range(1, PARTS)]


def pack_kernel(place, mask, diffusion, inverse, remap, mine, sent):
    rows, cols = mask.shape
    levels = inverse.shape[0]
    half, wide = levels // 2, cols // PARTS + 2
    wet = mask[...].astype(jnp.float32)
    nothing = jnp.zeros((1, rows), jnp.float32)
    folded = jnp.concatenate([inverse[:half, :], inverse[half:, :]], axis=1)
    for pack, part in ((mine, place[0]), (sent, place[0] ^ 2)):
        for slot, plane in enumerate((wet.T, (wet * diffusion[...]).T)):
            block = jnp.concatenate([nothing, plane, nothing], axis=0)
            for at in range(PARTS):

                @pl.when(part == at)
                def _():
                    first = at * (wide - 2)
                    pack[slot * wide : (slot + 1) * wide, :] = block[first : first + wide]

        pack[2 * wide : 2 * wide + half, :] = folded
        pack[2 * wide + half :, :] = remap[...].astype(jnp.float32)


def parameters(place, mask, diffusion, inverse, remap):
    rows, cols = mask.shape
    count = 2 * (cols // PARTS + 2) + inverse.shape[0] // 2 + 1
    pack = jax.ShapeDtypeStruct((count, rows), jnp.float32)
    return pl.pallas_call(
        pack_kernel,
        out_shape=[pack, pack],
        in_specs=[SMEM] + [VMEM] * 4,
        out_specs=[VMEM, VMEM],
        name="parameters",
    )(place, mask, diffusion, inverse, remap)


def split_kernel(place, field, p0, p1, p2, p3, q2, ends, turned):
    levels, rows, cols = field.shape
    width = cols // PARTS
    turned[0] = jnp.zeros((levels, rows), jnp.float32)
    turned[cols + 1] = jnp.zeros((levels, rows), jnp.float32)
    flat = turned.reshape((cols + 2) * levels, rows)
    for level in range(levels):
        flat[pl.ds(levels + level, cols, stride=levels), :] = field[level].T
    for bits, part in ((0, p0), (1, p1), (2, p2), (3, p3)):
        part[...] = turned[pl.ds((place[0] ^ bits) * width, part.shape[0])]
    q2[...] = turned[pl.ds((place[0] ^ 2) * width + p2.shape[0], q2.shape[0])]
    ends[0] = turned[1]
    ends[1] = turned[cols]


def split_columns(place, field):
    levels, rows, cols = field.shape
    wide = cols // PARTS + 2
    counts = [wide, wide, FIRST, wide, wide - FIRST, 2]
    return pl.pallas_call(
        split_kernel,
        grid=(levels // BLOCK,),
        out_shape=[jax.ShapeDtypeStruct((count, levels, rows), jnp.float32) for count in counts],
        in_specs=[SMEM, pl.BlockSpec((BLOCK, rows, cols), lambda i: (i, 0, 0))],
        out_specs=[pl.BlockSpec((count, BLOCK, rows), lambda i: (0, i, 0)) for count in counts],
        scratch_shapes=[pltpu.VMEM((cols + 2, BLOCK, rows), jnp.float32)],
        name="split_columns",
    )(place, field)


def border_kernel(place, lent_rows, field, ends, gain, borders, held, arrivals):
    levels, rows, cols = field.shape
    wanted = (0, rows - 1, lent_rows[0], lent_rows[rows - 1])
    copies = [
        pltpu.make_async_copy(field.at[:, pl.ds(row, 1), :], held.at[slot], arrivals.at[slot])
        for slot, row in enumerate(wanted)
    ]
    for copy in copies:
        copy.start()
    for copy in copies:
        copy.wait()
    component = place[0] // 2
    for at in range(PARTS):
        lent = (component != at // 2).astype(jnp.int32)
        for slot in range(2):
            borders[at, slot * levels : (slot + 1) * levels, :] = held[2 * lent + slot].reshape(levels, cols)
            borders[at, (2 + slot) * levels : (3 + slot) * levels, :] = ends[slot]
        borders[at, 4 * levels :, :] = jnp.zeros((1, rows), jnp.float32)
        borders[at, 4 * levels :, :levels] = gain[...]


def side_borders(place, lent_rows, field, ends, gain):
    levels, rows, cols = field.shape
    return pl.pallas_call(
        border_kernel,
        out_shape=jax.ShapeDtypeStruct((PARTS, 4 * levels + 1, rows), jnp.float32),
        in_specs=[SMEM, SMEM, pl.BlockSpec(memory_space=pl.ANY), VMEM, VMEM],
        out_specs=VMEM,
        scratch_shapes=[pltpu.VMEM((4, levels, 1, cols), jnp.float32), pltpu.SemaphoreType.DMA((4,))],
        name="side_borders",
    )(place, lent_rows, field, ends, gain)


def join_kernel(place, p0, p1, p2, p3, sides, top_bottom, out, turned):
    levels, rows, cols = out.shape
    width = cols // PARTS
    for bits, part in enumerate((p0, p1, p2, p3)):
        turned[pl.ds((place[0] ^ bits) * width, width)] = part[...]
    for part in range(PARTS):
        for side in range(2):
            at = part * width + side * (width - 1)
            turned[at] = turned[at] + sides[part, side]
    flat = turned.reshape(cols * levels, rows)
    row = lax.broadcasted_iota(jnp.int32, (rows, cols), 0)
    for level in range(levels):
        plane = flat[pl.ds(level, cols, stride=levels), :].T
        top = top_bottom[0, level : level + 1, :]
        bottom = top_bottom[1, level : level + 1, :]
        out[level] = plane + jnp.where(row == 0, top, jnp.where(row == rows - 1, bottom, 0.0))


def join_columns(place, parts, sides, top_bottom):
    width, levels, rows = parts[0].shape
    cols = width * PARTS
    return pl.pallas_call(
        join_kernel,
        grid=(levels // BLOCK,),
        out_shape=jax.ShapeDtypeStruct((levels, rows, cols), jnp.float32),
        in_specs=[SMEM]
        + [pl.BlockSpec((width, BLOCK, rows), lambda i: (0, i, 0))] * PARTS
        + [
            pl.BlockSpec((PARTS, 2, BLOCK, rows), lambda i: (0, 0, i, 0)),
            pl.BlockSpec((2, BLOCK, cols), lambda i: (0, i, 0)),
        ],
        out_specs=pl.BlockSpec((BLOCK, rows, cols), lambda i: (i, 0, 0)),
        scratch_shapes=[pltpu.VMEM((cols, BLOCK, rows), jnp.float32)],
        compiler_params=pltpu.CompilerParams(vmem_limit_bytes=16 << 20),
        name="join_columns",
    )(place, *parts, sides, top_bottom)


def halves(value):
    high = value.astype(jnp.bfloat16)
    low = (value - high.astype(jnp.float32)).astype(jnp.bfloat16)
    return high, low


def picked(value, index):
    return jnp.take_along_axis(value, index, axis=1, mode="promise_in_bounds")


def steps_kernel(
    place, p0, p1, p2, p3, q2, my_pack, other_pack, gains, halos,
    o0, o1, o2, o3, edges, column, state,
):
    outs = (o0, o1, o2, o3)
    wide, half, rows = p0.shape
    spot, width = place[0], wide - 2
    packs = (my_pack, other_pack)
    at_once, few = 16, 8
    levels = 2 * half
    lane = lax.broadcasted_iota(jnp.int32, (levels, rows), 1)
    mixes, picks = [], []
    for pack in packs:
        folded = pack[2 * wide : 2 * wide + half, :].T
        mix = jnp.concatenate([folded[:levels], folded[levels:]], axis=1)
        turned = jnp.concatenate([mix[half:], mix[:half]], axis=0)
        turned = jnp.concatenate([turned[:, half:], turned[:, :half]], axis=1)
        high, low = halves(jnp.where(spot % 2 == 0, mix, turned))
        mixes.append(jnp.concatenate([high, low, high], axis=1))
        pick = pack[2 * wide + half :, :].astype(jnp.int32)
        picks.append(jnp.broadcast_to(pick, (levels, rows)))

    def joined(blocks, comp, *at):
        return jnp.concatenate(
            [blocks[(spot ^ (2 * comp + part),) + at] for part in range(2)], axis=0
        )

    gain = []
    for comp in range(2):
        parts_of = [jnp.broadcast_to(gains[spot ^ (2 * comp + part)], (rows, rows)).T for part in range(2)]
        gain.append(jnp.concatenate([block[:half] for block in parts_of], axis=0))

    def solve(load, first, store, count):
        for comp in range(2):
            rights = []
            for at in range(count):
                coupled = load(comp, first + at)
                coupled = coupled + gain[comp] * picked(load(1 - comp, first + at), picks[comp])
                high, low = halves(coupled)
                rights.append(jnp.concatenate([high, high, low], axis=0))
            for at in range(0, count, 2):
                pair = jnp.concatenate(rights[at : at + 2], axis=1)
                solved = jnp.dot(mixes[comp], pair, preferred_element_type=jnp.float32)
                for side in range(2):
                    column[comp, store + at + side] = solved[:, side * rows : (side + 1) * rows]

    def flux(comp, at):
        return column[comp, at] * packs[comp][pl.ds(wide + at, 1), :]

    def lap(around, ends):
        mid = around[1]
        above = jnp.where(lane == 0, ends, pltpu.roll(mid, 1, 1))
        below = jnp.where(lane == rows - 1, ends, pltpu.roll(mid, rows - 1, 1))
        return above + below + around[0] + around[2] - 4.0 * mid

    def arrived(comp, at):
        if comp == 0:
            blocks = [p0[at], p1[at]]
        else:
            blocks = [p2[at] if at < FIRST else q2[at - FIRST], p3[at]]
        return jnp.concatenate(blocks, axis=0)

    for first in range(0, wide, at_once):
        solve(arrived, first, first, min(at_once, wide - first))
    tops = []
    for comp in range(2):
        folded = [halos[spot ^ (2 * comp + part), half:] for part in range(2)]
        folded = [block[:, first : first + 2 * width] for block in folded for first in (0, 2 * width)]
        ends = jnp.concatenate(folded, axis=0)
        tops.append(jnp.concatenate([ends, ends], axis=1))
    outer = []
    for comp in range(2):
        across = joined(halos, comp, slice(0, half))
        outer.append(
            (
                jnp.where(place[0] == 0, across, flux(comp, 0)),
                jnp.where(place[0] == PARTS - 1, across, flux(comp, width + 1)),
            )
        )

    def spread_first(first, left, right):
        for comp in range(2):
            fluxes = [flux(comp, first + at) for at in range(few + 2)]
            if left:
                fluxes[0] = outer[comp][0]
            if right:
                fluxes[-1] = outer[comp][1]
            for at in range(few):
                j = first + at
                ends = picked(tops[comp], jnp.where(lane == 0, j, j + width))
                total = column[comp, j + 1] + lap(fluxes[at : at + 3], ends)
                state[comp, j] = packs[comp][pl.ds(j + 1, 1), :] * total

    for first in range(0, width, few):
        spread_first(first, first == 0, first + few == width)

    def held(comp, at):
        return state[comp, at]

    for first in range(0, width, at_once):
        solve(held, first, first + 1, at_once)
    for comp in range(2):
        column[comp, 0] = jnp.zeros((levels, rows), jnp.float32)
        column[comp, width + 1] = jnp.zeros((levels, rows), jnp.float32)

    def second_spread(step, carry):
        kept = []
        for comp in range(2):
            first = step * few
            fluxes = [flux(comp, first + at) for at in range(few + 2)]
            both = carry[comp]
            for at in range(few):
                j = first + at
                total = column[comp, j + 1] + lap(fluxes[at : at + 3], 0.0)
                done = packs[comp][pl.ds(j + 1, 1), :] * total
                outs[2 * comp][j] = done[:half]
                outs[2 * comp + 1][j] = done[half:]
                ends = picked(fluxes[at + 1], jnp.where(lane == j, 0, rows - 1))
                both = jnp.where((lane == j) | (lane == j + width), ends, both)
            kept.append(both)
        return tuple(kept)

    empty = jnp.zeros((levels, rows), jnp.float32)
    both = (empty, empty)
    for step in range(width // few):
        both = second_spread(step, both)
    for comp in range(2):
        for part in range(2):
            to, span = spot ^ (2 * comp + part), slice(part * half, (part + 1) * half)
            edges[to, :half] = flux(comp, 1)[span]
            edges[to, half : 2 * half] = flux(comp, width)[span]
            ends = both[comp][span, : 2 * width]
            edges[to, 2 * half :] = jnp.concatenate([ends[: half // 2], ends[half // 2 :]], axis=1)


def two_steps(place, parts, packs, gains, halos):
    wide, half, rows = parts[0].shape
    width = wide - 2
    part = pltpu.HBM((width, half, rows), jnp.float32)
    *results, edges = pl.pallas_call(
        steps_kernel,
        out_shape=[part] * PARTS + [pltpu.VMEM((PARTS, 2 * half + half // 2, rows), jnp.float32)],
        in_specs=[SMEM] + [VMEM] * 9,
        out_specs=[VMEM] * (PARTS + 1),
        scratch_shapes=[
            pltpu.VMEM((2, wide, 2 * half, rows), jnp.float32),
            pltpu.VMEM((2, width, 2 * half, rows), jnp.float32),
        ],
        compiler_params=pltpu.CompilerParams(vmem_limit_bytes=24 << 20),
        name="two_steps",
    )(place, *map(in_vmem, parts), *packs, gains, halos)
    return results, edges


def tile_halo(edges, nbr_tile, nbr_side, nbr_flip):
    every = lax.all_gather(edges, "tile", axis=0)
    found = every[jnp.maximum(nbr_tile, 0), nbr_side]
    turned = jnp.where((nbr_flip == 1)[:, None, None], found[..., ::-1], found)
    return jnp.where((nbr_tile >= 0)[:, None, None], turned, jnp.float32(0.0))


def on_device(
    adjoint, diffusion, wet_mask, remap, coupling, vert_inverse, nbr_tile, nbr_side, nbr_flip
):
    field = adjoint[0, 0]
    half, rows, cols = field.shape
    width = cols // PARTS
    component, level_at = lax.axis_index("sect"), lax.axis_index("lev")
    spot = component * 2 + level_at
    place = spot[None].astype(jnp.int32)
    near = (nbr_tile[0], nbr_side[0], nbr_flip[0])
    inverse = vert_inverse[0, 0]
    my_rows = remap[0, 0]

    own_pack, sent = parameters(place, wet_mask[0, 0], diffusion[0, 0], inverse, remap[0])
    packs = [own_pack, exchanged(sent, 2)]
    other_rows = packs[1][-1].astype(jnp.int32)

    mine, beside, ahead, far, rest, ends = split_columns(place, field)
    ahead = exchanged(ahead, 2)
    borders = side_borders(place, other_rows, field, ends, coupling)
    beside, far, rest, borders, wet_mask, diffusion, inverse = lax.optimization_barrier(
        (beside, far, rest, borders, wet_mask, diffusion, inverse)
    )
    borders = traded(borders)
    parts = [mine, exchanged(beside, 1), ahead, exchanged(far, 3), exchanged(rest, 2)]

    wet = wet_mask[0, 0].astype(jnp.float32)
    spread = wet * diffusion[0, 0]

    gain_rows = borders[:, -1:]
    gains = borders[:, -1, :half].reshape(2, 2 * half)
    borders = borders[:, :-1].reshape(2, 2, 4, half, rows)
    borders = borders.transpose(0, 2, 1, 3, 4).reshape(2, 4, 2 * half, rows)
    own, pulled = [jnp.where(component == comp, borders[0], borders[1]) for comp in range(2)]
    my_gain = jnp.where(component == 0, gains[0], gains[1])
    choose = (jnp.arange(rows)[:, None] == my_rows[None, :]).astype(jnp.float32)
    pulled_columns = jnp.einsum("slq,qr->slr", pulled[2:], choose, precision=HIGHEST)
    coupled = own + my_gain[None, :, None] * jnp.concatenate([pulled[:2], pulled_columns])
    mine = lax.dynamic_slice_in_dim(inverse, level_at * half, half, 1)
    solved = jnp.einsum("kl,skx->slx", mine, coupled, precision=HIGHEST)

    def border(plane):
        return jnp.stack([plane[0], plane[rows - 1], plane[:, 0], plane[:, cols - 1]])[:, None, :]

    halo = tile_halo(solved * border(spread), *near)
    blocks = []
    for part in range(PARTS):
        span = slice(part * width, (part + 1) * width)
        ends = jnp.concatenate([halo[0][:, span], halo[1][:, span]], axis=1)
        ends = jnp.concatenate([ends[: half // 2], ends[half // 2 :]], axis=1)
        blocks.append(jnp.concatenate([halo[2] if part == 0 else halo[3], ends]))
    halos = traded(jnp.stack(blocks))

    results, edges = two_steps(place, parts, packs, gain_rows, halos)

    edges = traded(edges)
    results = all_exchanged(results)
    starts, stops, folded = edges[:, :half], edges[:, half : 2 * half], edges[:, 2 * half :]
    folded = folded.reshape(PARTS, half // 2, 2, 2, width).transpose(3, 2, 1, 0, 4).reshape(2, half, cols)
    halo = tile_halo(jnp.concatenate([folded, starts[:1], stops[PARTS - 1 :]]), *near)
    sides = []
    for part in range(PARTS):
        left = halo[2] if part == 0 else stops[part - 1]
        right = halo[3] if part == PARTS - 1 else starts[part + 1]
        sides.append(
            jnp.stack([left * wet[:, part * width], right * wet[:, (part + 1) * width - 1]])
        )
    top_bottom = jnp.stack([halo[0] * wet[0], halo[1] * wet[rows - 1]])
    return join_columns(place, results, jnp.stack(sides), top_bottom)[None, None]


def solution(mesh):
    in_specs = (
        P("sect", "tile", "lev", None, None),
        P("sect", "tile", None, None),
        P("sect", "tile", None, None),
        P("sect", "tile", None),
        P("sect", "lev"),
        P("sect", "tile", None, None),
        P("tile", None),
        P("tile", None),
        P("tile", None),
    )
    out_specs = P("sect", "tile", "lev", None, None)
    return jax.shard_map(
        on_device, mesh=mesh, in_specs=in_specs, out_specs=out_specs, check_vma=False
    )
```

```python
import jax
import jax.numpy as jnp
from jax import lax
from jax.experimental import pallas as pl
from jax.experimental.pallas import tpu as pltpu
from jax.sharding import PartitionSpec as P

Z = ("sect", "lev")
PARTS = 4
BLOCK = 16
JOIN_BLOCK = 8
FIRST = 16
HIGHEST = lax.Precision.HIGHEST
SMEM = pl.BlockSpec(memory_space=pltpu.SMEM)
VMEM = pl.BlockSpec(memory_space=pltpu.VMEM)


def in_vmem(block):
    return pltpu.with_memory_space_constraint(block, pltpu.VMEM)


def traded(blocks):
    return lax.all_to_all(blocks, Z, 0, 0)


def exchanged(block, bits):
    return lax.ppermute(block, Z, [(at, at ^ bits) for at in range(PARTS)])


def all_exchanged(blocks):
    return [blocks[0]] + [exchanged(blocks[bits], bits) for bits in range(1, PARTS)]


def pack_kernel(place, mask, diffusion, inverse, remap, mine, sent):
    rows, cols = mask.shape
    levels = inverse.shape[0]
    half, wide = levels // 2, cols // PARTS + 2
    wet = mask[...].astype(jnp.float32)
    nothing = jnp.zeros((1, rows), jnp.float32)
    folded = jnp.concatenate([inverse[:half, :], inverse[half:, :]], axis=1)
    for pack, part in ((mine, place[0]), (sent, place[0] ^ 2)):
        for slot, plane in enumerate((wet.T, (wet * diffusion[...]).T)):
            block = jnp.concatenate([nothing, plane, nothing], axis=0)
            for at in range(PARTS):

                @pl.when(part == at)
                def _():
                    first = at * (wide - 2)
                    pack[slot * wide : (slot + 1) * wide, :] = block[first : first + wide]

        pack[2 * wide : 2 * wide + half, :] = folded
        pack[2 * wide + half :, :] = remap[...].astype(jnp.float32)


def parameters(place, mask, diffusion, inverse, remap):
    rows, cols = mask.shape
    count = 2 * (cols // PARTS + 2) + inverse.shape[0] // 2 + 1
    pack = jax.ShapeDtypeStruct((count, rows), jnp.float32)
    return pl.pallas_call(
        pack_kernel,
        out_shape=[pack, pack],
        in_specs=[SMEM] + [VMEM] * 4,
        out_specs=[VMEM, VMEM],
        name="parameters",
    )(place, mask, diffusion, inverse, remap)


def split_kernel(place, field, p0, p1, p2, p3, q2, ends, turned):
    levels, rows, cols = field.shape
    width = cols // PARTS
    turned[0] = jnp.zeros((levels, rows), jnp.float32)
    turned[cols + 1] = jnp.zeros((levels, rows), jnp.float32)
    flat = turned.reshape((cols + 2) * levels, rows)
    for level in range(levels):
        flat[pl.ds(levels + level, cols, stride=levels), :] = field[level].T
    for bits, part in ((0, p0), (1, p1), (2, p2), (3, p3)):
        part[...] = turned[pl.ds((place[0] ^ bits) * width, part.shape[0])]
    q2[...] = turned[pl.ds((place[0] ^ 2) * width + p2.shape[0], q2.shape[0])]
    ends[0] = turned[1]
    ends[1] = turned[cols]


def split_columns(place, field):
    levels, rows, cols = field.shape
    wide = cols // PARTS + 2
    counts = [wide, wide, FIRST, wide, wide - FIRST, 2]
    return pl.pallas_call(
        split_kernel,
        grid=(levels // BLOCK,),
        out_shape=[jax.ShapeDtypeStruct((count, levels, rows), jnp.float32) for count in counts],
        in_specs=[SMEM, pl.BlockSpec((BLOCK, rows, cols), lambda i: (i, 0, 0))],
        out_specs=[pl.BlockSpec((count, BLOCK, rows), lambda i: (0, i, 0)) for count in counts],
        scratch_shapes=[pltpu.VMEM((cols + 2, BLOCK, rows), jnp.float32)],
        name="split_columns",
    )(place, field)


def border_kernel(place, lent_rows, field, ends, gain, borders, held, arrivals):
    levels, rows, cols = field.shape
    wanted = (0, rows - 1, lent_rows[0], lent_rows[rows - 1])
    copies = [
        pltpu.make_async_copy(field.at[:, pl.ds(row, 1), :], held.at[slot], arrivals.at[slot])
        for slot, row in enumerate(wanted)
    ]
    for copy in copies:
        copy.start()
    for copy in copies:
        copy.wait()
    component = place[0] // 2
    for at in range(PARTS):
        lent = (component != at // 2).astype(jnp.int32)
        for slot in range(2):
            borders[at, slot * levels : (slot + 1) * levels, :] = held[2 * lent + slot].reshape(levels, cols)
            borders[at, (2 + slot) * levels : (3 + slot) * levels, :] = ends[slot]
        borders[at, 4 * levels :, :] = jnp.zeros((1, rows), jnp.float32)
        borders[at, 4 * levels :, :levels] = gain[...]


def side_borders(place, lent_rows, field, ends, gain):
    levels, rows, cols = field.shape
    return pl.pallas_call(
        border_kernel,
        out_shape=jax.ShapeDtypeStruct((PARTS, 4 * levels + 1, rows), jnp.float32),
        in_specs=[SMEM, SMEM, pl.BlockSpec(memory_space=pl.ANY), VMEM, VMEM],
        out_specs=VMEM,
        scratch_shapes=[pltpu.VMEM((4, levels, 1, cols), jnp.float32), pltpu.SemaphoreType.DMA((4,))],
        name="side_borders",
    )(place, lent_rows, field, ends, gain)


def join_kernel(place, p0, p1, p2, p3, sides, top_bottom, out, turned):
    levels, rows, cols = out.shape
    width = cols // PARTS
    for bits, part in enumerate((p0, p1, p2, p3)):
        turned[pl.ds((place[0] ^ bits) * width, width)] = part[...]
    for part in range(PARTS):
        for side in range(2):
            at = part * width + side * (width - 1)
            turned[at] = turned[at] + sides[part, side]
    flat = turned.reshape(cols * levels, rows)
    row = lax.broadcasted_iota(jnp.int32, (rows, cols), 0)
    for level in range(levels):
        plane = flat[pl.ds(level, cols, stride=levels), :].T
        top = top_bottom[0, level : level + 1, :]
        bottom = top_bottom[1, level : level + 1, :]
        out[level] = plane + jnp.where(row == 0, top, jnp.where(row == rows - 1, bottom, 0.0))


def join_columns(place, parts, sides, top_bottom):
    width, levels, rows = parts[0].shape
    cols = width * PARTS
    return pl.pallas_call(
        join_kernel,
        grid=(levels // JOIN_BLOCK,),
        out_shape=jax.ShapeDtypeStruct((levels, rows, cols), jnp.float32),
        in_specs=[SMEM]
        + [pl.BlockSpec((width, JOIN_BLOCK, rows), lambda i: (0, i, 0))] * PARTS
        + [
            pl.BlockSpec((PARTS, 2, JOIN_BLOCK, rows), lambda i: (0, 0, i, 0)),
            pl.BlockSpec((2, JOIN_BLOCK, cols), lambda i: (0, i, 0)),
        ],
        out_specs=pl.BlockSpec((JOIN_BLOCK, rows, cols), lambda i: (i, 0, 0)),
        scratch_shapes=[pltpu.VMEM((cols, JOIN_BLOCK, rows), jnp.float32)],
        compiler_params=pltpu.CompilerParams(vmem_limit_bytes=16 << 20),
        name="join_columns",
    )(place, *parts, sides, top_bottom)


def halves(value):
    high = value.astype(jnp.bfloat16)
    low = (value - high.astype(jnp.float32)).astype(jnp.bfloat16)
    return high, low


def picked(value, index):
    return jnp.take_along_axis(value, index, axis=1, mode="promise_in_bounds")


def steps_kernel(
    place, p0, p1, p2, p3, q2, my_pack, other_pack, gains, halos,
    o0, o1, o2, o3, edges, column, state,
):
    outs = (o0, o1, o2, o3)
    wide, half, rows = p0.shape
    spot, width = place[0], wide - 2
    packs = (my_pack, other_pack)
    at_once, few = 16, 8
    levels = 2 * half
    lane = lax.broadcasted_iota(jnp.int32, (levels, rows), 1)
    mixes, picks = [], []
    for pack in packs:
        folded = pack[2 * wide : 2 * wide + half, :].T
        mix = jnp.concatenate([folded[:levels], folded[levels:]], axis=1)
        turned = jnp.concatenate([mix[half:], mix[:half]], axis=0)
        turned = jnp.concatenate([turned[:, half:], turned[:, :half]], axis=1)
        high, low = halves(jnp.where(spot % 2 == 0, mix, turned))
        mixes.append(jnp.concatenate([high, low, high], axis=1))
        pick = pack[2 * wide + half :, :].astype(jnp.int32)
        picks.append(jnp.broadcast_to(pick, (levels, rows)))

    def joined(blocks, comp, *at):
        return jnp.concatenate(
            [blocks[(spot ^ (2 * comp + part),) + at] for part in range(2)], axis=0
        )

    gain = []
    for comp in range(2):
        parts_of = [jnp.broadcast_to(gains[spot ^ (2 * comp + part)], (rows, rows)).T for part in range(2)]
        gain.append(jnp.concatenate([block[:half] for block in parts_of], axis=0))

    def solve(load, first, store, count):
        for comp in range(2):
            rights = []
            for at in range(count):
                coupled = load(comp, first + at)
                coupled = coupled + gain[comp] * picked(load(1 - comp, first + at), picks[comp])
                high, low = halves(coupled)
                rights.append(jnp.concatenate([high, high, low], axis=0))
            for at in range(0, count, 2):
                pair = jnp.concatenate(rights[at : at + 2], axis=1)
                solved = jnp.dot(mixes[comp], pair, preferred_element_type=jnp.float32)
                for side in range(2):
                    column[comp, store + at + side] = solved[:, side * rows : (side + 1) * rows]

    def flux(comp, at):
        return column[comp, at] * packs[comp][pl.ds(wide + at, 1), :]

    def lap(around, ends):
        mid = around[1]
        above = jnp.where(lane == 0, ends, pltpu.roll(mid, 1, 1))
        below = jnp.where(lane == rows - 1, ends, pltpu.roll(mid, rows - 1, 1))
        return above + below + around[0] + around[2] - 4.0 * mid

    def arrived(comp, at):
        if comp == 0:
            blocks = [p0[at], p1[at]]
        else:
            blocks = [p2[at] if at < FIRST else q2[at - FIRST], p3[at]]
        return jnp.concatenate(blocks, axis=0)

    for first in range(0, wide, at_once):
        solve(arrived, first, first, min(at_once, wide - first))
    tops = []
    for comp in range(2):
        folded = [halos[spot ^ (2 * comp + part), half:] for part in range(2)]
        folded = [block[:, first : first + 2 * width] for block in folded for first in (0, 2 * width)]
        ends = jnp.concatenate(folded, axis=0)
        tops.append(jnp.concatenate([ends, ends], axis=1))
    outer = []
    for comp in range(2):
        across = joined(halos, comp, slice(0, half))
        outer.append(
            (
                jnp.where(place[0] == 0, across, flux(comp, 0)),
                jnp.where(place[0] == PARTS - 1, across, flux(comp, width + 1)),
            )
        )

    def spread_first(first, left, right):
        for comp in range(2):
            fluxes = [flux(comp, first + at) for at in range(few + 2)]
            if left:
                fluxes[0] = outer[comp][0]
            if right:
                fluxes[-1] = outer[comp][1]
            for at in range(few):
                j = first + at
                ends = picked(tops[comp], jnp.where(lane == 0, j, j + width))
                total = column[comp, j + 1] + lap(fluxes[at : at + 3], ends)
                state[comp, j] = packs[comp][pl.ds(j + 1, 1), :] * total

    for first in range(0, width, few):
        spread_first(first, first == 0, first + few == width)

    def held(comp, at):
        return state[comp, at]

    for first in range(0, width, at_once):
        solve(held, first, first + 1, at_once)
    for comp in range(2):
        column[comp, 0] = jnp.zeros((levels, rows), jnp.float32)
        column[comp, width + 1] = jnp.zeros((levels, rows), jnp.float32)

    def second_spread(step, carry):
        kept = []
        for comp in range(2):
            first = step * few
            fluxes = [flux(comp, first + at) for at in range(few + 2)]
            both = carry[comp]
            for at in range(few):
                j = first + at
                total = column[comp, j + 1] + lap(fluxes[at : at + 3], 0.0)
                done = packs[comp][pl.ds(j + 1, 1), :] * total
                outs[2 * comp][j] = done[:half]
                outs[2 * comp + 1][j] = done[half:]
                ends = picked(fluxes[at + 1], jnp.where(lane == j, 0, rows - 1))
                both = jnp.where((lane == j) | (lane == j + width), ends, both)
            kept.append(both)
        return tuple(kept)

    empty = jnp.zeros((levels, rows), jnp.float32)
    both = (empty, empty)
    for step in range(width // few):
        both = second_spread(step, both)
    for comp in range(2):
        for part in range(2):
            to, span = spot ^ (2 * comp + part), slice(part * half, (part + 1) * half)
            edges[to, :half] = flux(comp, 1)[span]
            edges[to, half : 2 * half] = flux(comp, width)[span]
            ends = both[comp][span, : 2 * width]
            edges[to, 2 * half :] = jnp.concatenate([ends[: half // 2], ends[half // 2 :]], axis=1)


def two_steps(place, parts, packs, gains, halos):
    wide, half, rows = parts[0].shape
    width = wide - 2
    part = pltpu.HBM((width, half, rows), jnp.float32)
    *results, edges = pl.pallas_call(
        steps_kernel,
        out_shape=[part] * 2 + [pltpu.VMEM((width, half, rows), jnp.float32)] * 2 + [pltpu.VMEM((PARTS, 2 * half + half // 2, rows), jnp.float32)],
        in_specs=[SMEM] + [VMEM] * 9,
        out_specs=[VMEM] * (PARTS + 1),
        scratch_shapes=[
            pltpu.VMEM((2, wide, 2 * half, rows), jnp.float32),
            pltpu.VMEM((2, width, 2 * half, rows), jnp.float32),
        ],
        compiler_params=pltpu.CompilerParams(vmem_limit_bytes=24 << 20),
        name="two_steps",
    )(place, *map(in_vmem, parts), *packs, gains, halos)
    return results, edges


def tile_halo(edges, nbr_tile, nbr_side, nbr_flip):
    every = lax.all_gather(edges, "tile", axis=0)
    found = every[jnp.maximum(nbr_tile, 0), nbr_side]
    turned = jnp.where((nbr_flip == 1)[:, None, None], found[..., ::-1], found)
    return jnp.where((nbr_tile >= 0)[:, None, None], turned, jnp.float32(0.0))


def on_device(
    adjoint, diffusion, wet_mask, remap, coupling, vert_inverse, nbr_tile, nbr_side, nbr_flip
):
    field = adjoint[0, 0]
    half, rows, cols = field.shape
    width = cols // PARTS
    component, level_at = lax.axis_index("sect"), lax.axis_index("lev")
    spot = component * 2 + level_at
    place = spot[None].astype(jnp.int32)
    near = (nbr_tile[0], nbr_side[0], nbr_flip[0])
    inverse = vert_inverse[0, 0]
    my_rows = remap[0, 0]

    own_pack, sent = parameters(place, wet_mask[0, 0], diffusion[0, 0], inverse, remap[0])
    packs = [own_pack, exchanged(sent, 2)]
    other_rows = packs[1][-1].astype(jnp.int32)

    mine, beside, ahead, far, rest, ends = split_columns(place, field)
    ahead = exchanged(ahead, 2)
    borders = side_borders(place, other_rows, field, ends, coupling)
    beside, far, rest, borders, wet_mask, diffusion, inverse = lax.optimization_barrier(
        (beside, far, rest, borders, wet_mask, diffusion, inverse)
    )
    borders = traded(borders)
    parts = [mine, exchanged(beside, 1), ahead, exchanged(far, 3), exchanged(rest, 2)]

    wet = wet_mask[0, 0].astype(jnp.float32)
    spread = wet * diffusion[0, 0]

    gain_rows = borders[:, -1:]
    gains = borders[:, -1, :half].reshape(2, 2 * half)
    borders = borders[:, :-1].reshape(2, 2, 4, half, rows)
    borders = borders.transpose(0, 2, 1, 3, 4).reshape(2, 4, 2 * half, rows)
    own, pulled = [jnp.where(component == comp, borders[0], borders[1]) for comp in range(2)]
    my_gain = jnp.where(component == 0, gains[0], gains[1])
    choose = (jnp.arange(rows)[:, None] == my_rows[None, :]).astype(jnp.float32)
    pulled_columns = jnp.einsum("slq,qr->slr", pulled[2:], choose, precision=HIGHEST)
    coupled = own + my_gain[None, :, None] * jnp.concatenate([pulled[:2], pulled_columns])
    mine = lax.dynamic_slice_in_dim(inverse, level_at * half, half, 1)
    solved = jnp.einsum("kl,skx->slx", mine, coupled, precision=HIGHEST)

    def border(plane):
        return jnp.stack([plane[0], plane[rows - 1], plane[:, 0], plane[:, cols - 1]])[:, None, :]

    halo = tile_halo(solved * border(spread), *near)
    blocks = []
    for part in range(PARTS):
        span = slice(part * width, (part + 1) * width)
        ends = jnp.concatenate([halo[0][:, span], halo[1][:, span]], axis=1)
        ends = jnp.concatenate([ends[: half // 2], ends[half // 2 :]], axis=1)
        blocks.append(jnp.concatenate([halo[2] if part == 0 else halo[3], ends]))
    halos = traded(jnp.stack(blocks))

    results, edges = two_steps(place, parts, packs, gain_rows, halos)

    edges = traded(edges)
    results = all_exchanged(results)
    starts, stops, folded = edges[:, :half], edges[:, half : 2 * half], edges[:, 2 * half :]
    folded = folded.reshape(PARTS, half // 2, 2, 2, width).transpose(3, 2, 1, 0, 4).reshape(2, half, cols)
    halo = tile_halo(jnp.concatenate([folded, starts[:1], stops[PARTS - 1 :]]), *near)
    sides = []
    for part in range(PARTS):
        left = halo[2] if part == 0 else stops[part - 1]
        right = halo[3] if part == PARTS - 1 else starts[part + 1]
        sides.append(
            jnp.stack([left * wet[:, part * width], right * wet[:, (part + 1) * width - 1]])
        )
    top_bottom = jnp.stack([halo[0] * wet[0], halo[1] * wet[rows - 1]])
    return join_columns(place, results, jnp.stack(sides), top_bottom)[None, None]


def solution(mesh):
    in_specs = (
        P("sect", "tile", "lev", None, None),
        P("sect", "tile", None, None),
        P("sect", "tile", None, None),
        P("sect", "tile", None),
        P("sect", "lev"),
        P("sect", "tile", None, None),
        P("tile", None),
        P("tile", None),
        P("tile", None),
    )
    out_specs = P("sect", "tile", "lev", None, None)
    return jax.shard_map(
        on_device, mesh=mesh, in_specs=in_specs, out_specs=out_specs, check_vma=False
    )
```

```python
import jax
import jax.numpy as jnp
from jax import lax
from jax.experimental import pallas as pl
from jax.experimental.pallas import tpu as pltpu
from jax.sharding import PartitionSpec as P

Z = ("sect", "lev")
PARTS = 4
BLOCK = 16
JOIN_BLOCK = 8
FIRST = 16
HIGHEST = lax.Precision.HIGHEST
SMEM = pl.BlockSpec(memory_space=pltpu.SMEM)
VMEM = pl.BlockSpec(memory_space=pltpu.VMEM)


def in_vmem(block):
    return pltpu.with_memory_space_constraint(block, pltpu.VMEM)


def traded(blocks):
    return lax.all_to_all(blocks, Z, 0, 0)


def exchanged(block, bits):
    return lax.ppermute(block, Z, [(at, at ^ bits) for at in range(PARTS)])


def all_exchanged(blocks):
    return [blocks[0]] + [exchanged(blocks[bits], bits) for bits in range(1, PARTS)]


def pack_kernel(place, mask, diffusion, inverse, remap, mine, sent):
    rows, cols = mask.shape
    levels = inverse.shape[0]
    half, wide = levels // 2, cols // PARTS + 2
    wet = mask[...].astype(jnp.float32)
    nothing = jnp.zeros((1, rows), jnp.float32)
    folded = jnp.concatenate([inverse[:half, :], inverse[half:, :]], axis=1)
    for pack, part in ((mine, place[0]), (sent, place[0] ^ 2)):
        for slot, plane in enumerate((wet.T, (wet * diffusion[...]).T)):
            block = jnp.concatenate([nothing, plane, nothing], axis=0)
            for at in range(PARTS):

                @pl.when(part == at)
                def _():
                    first = at * (wide - 2)
                    pack[slot * wide : (slot + 1) * wide, :] = block[first : first + wide]

        pack[2 * wide : 2 * wide + half, :] = folded
        pack[2 * wide + half :, :] = remap[...].astype(jnp.float32)


def parameters(place, mask, diffusion, inverse, remap):
    rows, cols = mask.shape
    count = 2 * (cols // PARTS + 2) + inverse.shape[0] // 2 + 1
    pack = jax.ShapeDtypeStruct((count, rows), jnp.float32)
    return pl.pallas_call(
        pack_kernel,
        out_shape=[pack, pack],
        in_specs=[SMEM] + [VMEM] * 4,
        out_specs=[VMEM, VMEM],
        name="parameters",
    )(place, mask, diffusion, inverse, remap)


def split_kernel(place, field, p0, p1, p2, p3, q2, ends, turned):
    levels, rows, cols = field.shape
    width = cols // PARTS
    turned[0] = jnp.zeros((levels, rows), jnp.float32)
    turned[cols + 1] = jnp.zeros((levels, rows), jnp.float32)
    flat = turned.reshape((cols + 2) * levels, rows)
    for level in range(levels):
        flat[pl.ds(levels + level, cols, stride=levels), :] = field[level].T
    for bits, part in ((0, p0), (1, p1), (2, p2), (3, p3)):
        part[...] = turned[pl.ds((place[0] ^ bits) * width, part.shape[0])]
    q2[...] = turned[pl.ds((place[0] ^ 2) * width + p2.shape[0], q2.shape[0])]
    ends[0] = turned[1]
    ends[1] = turned[cols]


def split_columns(place, field):
    levels, rows, cols = field.shape
    wide = cols // PARTS + 2
    counts = [wide, wide, FIRST, wide, wide - FIRST, 2]
    return pl.pallas_call(
        split_kernel,
        grid=(levels // BLOCK,),
        out_shape=[jax.ShapeDtypeStruct((count, levels, rows), jnp.float32) for count in counts],
        in_specs=[SMEM, pl.BlockSpec((BLOCK, rows, cols), lambda i: (i, 0, 0))],
        out_specs=[pl.BlockSpec((count, BLOCK, rows), lambda i: (0, i, 0)) for count in counts],
        scratch_shapes=[pltpu.VMEM((cols + 2, BLOCK, rows), jnp.float32)],
        name="split_columns",
    )(place, field)


def border_kernel(place, lent_rows, field, ends, gain, borders, held, arrivals):
    levels, rows, cols = field.shape
    wanted = (0, rows - 1, lent_rows[0], lent_rows[rows - 1])
    copies = [
        pltpu.make_async_copy(field.at[:, pl.ds(row, 1), :], held.at[slot], arrivals.at[slot])
        for slot, row in enumerate(wanted)
    ]
    for copy in copies:
        copy.start()
    for copy in copies:
        copy.wait()
    component = place[0] // 2
    for at in range(PARTS):
        lent = (component != at // 2).astype(jnp.int32)
        for slot in range(2):
            borders[at, slot * levels : (slot + 1) * levels, :] = held[2 * lent + slot].reshape(levels, cols)
            borders[at, (2 + slot) * levels : (3 + slot) * levels, :] = ends[slot]
        borders[at, 4 * levels :, :] = jnp.zeros((1, rows), jnp.float32)
        borders[at, 4 * levels :, :levels] = gain[...]


def side_borders(place, lent_rows, field, ends, gain):
    levels, rows, cols = field.shape
    return pl.pallas_call(
        border_kernel,
        out_shape=jax.ShapeDtypeStruct((PARTS, 4 * levels + 1, rows), jnp.float32),
        in_specs=[SMEM, SMEM, pl.BlockSpec(memory_space=pl.ANY), VMEM, VMEM],
        out_specs=VMEM,
        scratch_shapes=[pltpu.VMEM((4, levels, 1, cols), jnp.float32), pltpu.SemaphoreType.DMA((4,))],
        name="side_borders",
    )(place, lent_rows, field, ends, gain)


def join_kernel(place, p0, p1, p2, p3, sides, top_bottom, out, turned):
    levels, rows, cols = out.shape
    width = cols // PARTS
    for bits, part in enumerate((p0, p1, p2, p3)):
        turned[pl.ds((place[0] ^ bits) * width, width)] = part[...]
    for part in range(PARTS):
        for side in range(2):
            at = part * width + side * (width - 1)
            turned[at] = turned[at] + sides[part, side]
    flat = turned.reshape(cols * levels, rows)
    row = lax.broadcasted_iota(jnp.int32, (rows, cols), 0)
    for level in range(levels):
        plane = flat[pl.ds(level, cols, stride=levels), :].T
        top = top_bottom[0, level : level + 1, :]
        bottom = top_bottom[1, level : level + 1, :]
        out[level] = plane + jnp.where(row == 0, top, jnp.where(row == rows - 1, bottom, 0.0))


def join_columns(place, parts, sides, top_bottom):
    width, levels, rows = parts[0].shape
    cols = width * PARTS
    return pl.pallas_call(
        join_kernel,
        grid=(levels // JOIN_BLOCK,),
        out_shape=jax.ShapeDtypeStruct((levels, rows, cols), jnp.float32),
        in_specs=[SMEM]
        + [pl.BlockSpec((width, JOIN_BLOCK, rows), lambda i: (0, i, 0))] * PARTS
        + [
            pl.BlockSpec((PARTS, 2, JOIN_BLOCK, rows), lambda i: (0, 0, i, 0)),
            pl.BlockSpec((2, JOIN_BLOCK, cols), lambda i: (0, i, 0)),
        ],
        out_specs=pl.BlockSpec((JOIN_BLOCK, rows, cols), lambda i: (i, 0, 0)),
        scratch_shapes=[pltpu.VMEM((cols, JOIN_BLOCK, rows), jnp.float32)],
        compiler_params=pltpu.CompilerParams(vmem_limit_bytes=16 << 20),
        name="join_columns",
    )(place, *parts, sides, top_bottom)


def halves(value):
    high = value.astype(jnp.bfloat16)
    low = (value - high.astype(jnp.float32)).astype(jnp.bfloat16)
    return high, low


def picked(value, index):
    return jnp.take_along_axis(value, index, axis=1, mode="promise_in_bounds")


def steps_kernel(
    place, p0, p1, p2, p3, q2, my_pack, other_pack, gains, halos,
    o0, o1, o2, o3, edges, column, state,
):
    outs = (o0, o1, o2, o3)
    wide, half, rows = p0.shape
    spot, width = place[0], wide - 2
    packs = (my_pack, other_pack)
    at_once, few = 16, 8
    levels = 2 * half
    lane = lax.broadcasted_iota(jnp.int32, (levels, rows), 1)
    mixes, picks = [], []
    for pack in packs:
        folded = pack[2 * wide : 2 * wide + half, :].T
        mix = jnp.concatenate([folded[:levels], folded[levels:]], axis=1)
        turned = jnp.concatenate([mix[half:], mix[:half]], axis=0)
        turned = jnp.concatenate([turned[:, half:], turned[:, :half]], axis=1)
        high, low = halves(jnp.where(spot % 2 == 0, mix, turned))
        mixes.append(jnp.concatenate([high, low, high], axis=1))
        pick = pack[2 * wide + half :, :].astype(jnp.int32)
        picks.append(jnp.broadcast_to(pick, (levels, rows)))

    def joined(blocks, comp, *at):
        return jnp.concatenate(
            [blocks[(spot ^ (2 * comp + part),) + at] for part in range(2)], axis=0
        )

    gain = []
    for comp in range(2):
        parts_of = [jnp.broadcast_to(gains[spot ^ (2 * comp + part)], (rows, rows)).T for part in range(2)]
        gain.append(jnp.concatenate([block[:half] for block in parts_of], axis=0))

    def solve(load, first, store, count):
        for comp in range(2):
            rights = []
            for at in range(count):
                coupled = load(comp, first + at)
                coupled = coupled + gain[comp] * picked(load(1 - comp, first + at), picks[comp])
                high, low = halves(coupled)
                rights.append(jnp.concatenate([high, high, low], axis=0))
            for at in range(0, count, 2):
                pair = jnp.concatenate(rights[at : at + 2], axis=1)
                solved = jnp.dot(mixes[comp], pair, preferred_element_type=jnp.float32)
                for side in range(2):
                    column[comp, store + at + side] = solved[:, side * rows : (side + 1) * rows]

    def flux(comp, at):
        return column[comp, at] * packs[comp][pl.ds(wide + at, 1), :]

    def lap(around, ends):
        mid = around[1]
        above = jnp.where(lane == 0, ends, pltpu.roll(mid, 1, 1))
        below = jnp.where(lane == rows - 1, ends, pltpu.roll(mid, rows - 1, 1))
        return above + below + around[0] + around[2] - 4.0 * mid

    def arrived(comp, at):
        if comp == 0:
            blocks = [p0[at], p1[at]]
        else:
            blocks = [p2[at] if at < FIRST else q2[at - FIRST], p3[at]]
        return jnp.concatenate(blocks, axis=0)

    for first in range(0, wide, at_once):
        solve(arrived, first, first, min(at_once, wide - first))
    tops = []
    for comp in range(2):
        folded = [halos[spot ^ (2 * comp + part), half:] for part in range(2)]
        folded = [block[:, first : first + 2 * width] for block in folded for first in (0, 2 * width)]
        ends = jnp.concatenate(folded, axis=0)
        tops.append(jnp.concatenate([ends, ends], axis=1))
    outer = []
    for comp in range(2):
        across = joined(halos, comp, slice(0, half))
        outer.append(
            (
                jnp.where(place[0] == 0, across, flux(comp, 0)),
                jnp.where(place[0] == PARTS - 1, across, flux(comp, width + 1)),
            )
        )

    def spread_first(first, left, right):
        for comp in range(2):
            fluxes = [flux(comp, first + at) for at in range(few + 2)]
            if left:
                fluxes[0] = outer[comp][0]
            if right:
                fluxes[-1] = outer[comp][1]
            for at in range(few):
                j = first + at
                ends = picked(tops[comp], jnp.where(lane == 0, j, j + width))
                total = column[comp, j + 1] + lap(fluxes[at : at + 3], ends)
                state[comp, j] = packs[comp][pl.ds(j + 1, 1), :] * total

    for first in range(0, width, few):
        spread_first(first, first == 0, first + few == width)

    def held(comp, at):
        return state[comp, at]

    for first in range(0, width, at_once):
        solve(held, first, first + 1, at_once)
    for comp in range(2):
        column[comp, 0] = jnp.zeros((levels, rows), jnp.float32)
        column[comp, width + 1] = jnp.zeros((levels, rows), jnp.float32)

    def second_spread(step, carry):
        kept = []
        for comp in range(2):
            first = step * few
            fluxes = [flux(comp, first + at) for at in range(few + 2)]
            both = carry[comp]
            for at in range(few):
                j = first + at
                total = column[comp, j + 1] + lap(fluxes[at : at + 3], 0.0)
                done = packs[comp][pl.ds(j + 1, 1), :] * total
                outs[2 * comp][j] = done[:half]
                outs[2 * comp + 1][j] = done[half:]
                ends = picked(fluxes[at + 1], jnp.where(lane == j, 0, rows - 1))
                both = jnp.where((lane == j) | (lane == j + width), ends, both)
            kept.append(both)
        return tuple(kept)

    empty = jnp.zeros((levels, rows), jnp.float32)
    both = (empty, empty)
    for step in range(width // few):
        both = second_spread(step, both)
    for comp in range(2):
        for part in range(2):
            to, span = spot ^ (2 * comp + part), slice(part * half, (part + 1) * half)
            edges[to, :half] = flux(comp, 1)[span]
            edges[to, half : 2 * half] = flux(comp, width)[span]
            ends = both[comp][span, : 2 * width]
            edges[to, 2 * half :] = jnp.concatenate([ends[: half // 2], ends[half // 2 :]], axis=1)


def two_steps(place, parts, packs, gains, halos):
    wide, half, rows = parts[0].shape
    width = wide - 2
    part = pltpu.HBM((width, half, rows), jnp.float32)
    *results, edges = pl.pallas_call(
        steps_kernel,
        out_shape=[part] * PARTS + [pltpu.VMEM((PARTS, 2 * half + half // 2, rows), jnp.float32)],
        in_specs=[SMEM] + [VMEM] * 9,
        out_specs=[VMEM] * (PARTS + 1),
        scratch_shapes=[
            pltpu.VMEM((2, wide, 2 * half, rows), jnp.float32),
            pltpu.VMEM((2, width, 2 * half, rows), jnp.float32),
        ],
        compiler_params=pltpu.CompilerParams(vmem_limit_bytes=24 << 20),
        name="two_steps",
    )(place, *map(in_vmem, parts), *packs, gains, halos)
    return results, edges


def tile_halo(edges, nbr_tile, nbr_side, nbr_flip):
    every = lax.all_gather(edges, "tile", axis=0)
    found = every[jnp.maximum(nbr_tile, 0), nbr_side]
    turned = jnp.where((nbr_flip == 1)[:, None, None], found[..., ::-1], found)
    return jnp.where((nbr_tile >= 0)[:, None, None], turned, jnp.float32(0.0))


def on_device(
    adjoint, diffusion, wet_mask, remap, coupling, vert_inverse, nbr_tile, nbr_side, nbr_flip
):
    field = adjoint[0, 0]
    half, rows, cols = field.shape
    width = cols // PARTS
    component, level_at = lax.axis_index("sect"), lax.axis_index("lev")
    spot = component * 2 + level_at
    place = spot[None].astype(jnp.int32)
    near = (nbr_tile[0], nbr_side[0], nbr_flip[0])
    inverse = vert_inverse[0, 0]
    my_rows = remap[0, 0]

    own_pack, sent = parameters(place, wet_mask[0, 0], diffusion[0, 0], inverse, remap[0])
    packs = [own_pack, exchanged(sent, 2)]
    other_rows = packs[1][-1].astype(jnp.int32)

    mine, beside, ahead, far, rest, ends = split_columns(place, field)
    ahead = exchanged(ahead, 2)
    borders = side_borders(place, other_rows, field, ends, coupling)
    beside, far, rest, borders, wet_mask, diffusion, inverse = lax.optimization_barrier(
        (beside, far, rest, borders, wet_mask, diffusion, inverse)
    )
    borders = traded(borders)
    parts = [mine, exchanged(beside, 1), ahead, exchanged(far, 3), exchanged(rest, 2)]

    wet = wet_mask[0, 0].astype(jnp.float32)
    spread = wet * diffusion[0, 0]

    gain_rows = borders[:, -1:]
    gains = borders[:, -1, :half].reshape(2, 2 * half)
    borders = borders[:, :-1].reshape(2, 2, 4, half, rows)
    borders = borders.transpose(0, 2, 1, 3, 4).reshape(2, 4, 2 * half, rows)
    own, pulled = [jnp.where(component == comp, borders[0], borders[1]) for comp in range(2)]
    my_gain = jnp.where(component == 0, gains[0], gains[1])
    choose = (jnp.arange(rows)[:, None] == my_rows[None, :]).astype(jnp.float32)
    pulled_columns = jnp.einsum("slq,qr->slr", pulled[2:], choose, precision=HIGHEST)
    coupled = own + my_gain[None, :, None] * jnp.concatenate([pulled[:2], pulled_columns])
    mine = lax.dynamic_slice_in_dim(inverse, level_at * half, half, 1)
    solved = jnp.einsum("kl,skx->slx", mine, coupled, precision=HIGHEST)

    def border(plane):
        return jnp.stack([plane[0], plane[rows - 1], plane[:, 0], plane[:, cols - 1]])[:, None, :]

    halo = tile_halo(solved * border(spread), *near)
    blocks = []
    for part in range(PARTS):
        span = slice(part * width, (part + 1) * width)
        ends = jnp.concatenate([halo[0][:, span], halo[1][:, span]], axis=1)
        ends = jnp.concatenate([ends[: half // 2], ends[half // 2 :]], axis=1)
        blocks.append(jnp.concatenate([halo[2] if part == 0 else halo[3], ends]))
    halos = traded(jnp.stack(blocks))

    results, edges = two_steps(place, parts, packs, gain_rows, halos)

    edges = traded(edges)
    results = all_exchanged(results)
    starts, stops, folded = edges[:, :half], edges[:, half : 2 * half], edges[:, 2 * half :]
    folded = folded.reshape(PARTS, half // 2, 2, 2, width).transpose(3, 2, 1, 0, 4).reshape(2, half, cols)
    halo = tile_halo(jnp.concatenate([folded, starts[:1], stops[PARTS - 1 :]]), *near)
    sides = []
    for part in range(PARTS):
        left = halo[2] if part == 0 else stops[part - 1]
        right = halo[3] if part == PARTS - 1 else starts[part + 1]
        sides.append(
            jnp.stack([left * wet[:, part * width], right * wet[:, (part + 1) * width - 1]])
        )
    top_bottom = jnp.stack([halo[0] * wet[0], halo[1] * wet[rows - 1]])
    return join_columns(place, results, jnp.stack(sides), top_bottom)[None, None]


def solution(mesh):
    in_specs = (
        P("sect", "tile", "lev", None, None),
        P("sect", "tile", None, None),
        P("sect", "tile", None, None),
        P("sect", "tile", None),
        P("sect", "lev"),
        P("sect", "tile", None, None),
        P("tile", None),
        P("tile", None),
        P("tile", None),
    )
    out_specs = P("sect", "tile", "lev", None, None)
    return jax.shard_map(
        on_device, mesh=mesh, in_specs=in_specs, out_specs=out_specs, check_vma=False
    )
```

```python
import jax
import jax.numpy as jnp
from jax import lax
from jax.experimental import pallas as pl
from jax.experimental.pallas import tpu as pltpu
from jax.sharding import PartitionSpec as P

Z = ("sect", "lev")
PARTS = 4
BLOCK = 16
FIRST = 16
HIGHEST = lax.Precision.HIGHEST
SMEM = pl.BlockSpec(memory_space=pltpu.SMEM)
VMEM = pl.BlockSpec(memory_space=pltpu.VMEM)


def in_vmem(block):
    return pltpu.with_memory_space_constraint(block, pltpu.VMEM)


def traded(blocks):
    return lax.all_to_all(blocks, Z, 0, 0)


def exchanged(block, bits):
    return lax.ppermute(block, Z, [(at, at ^ bits) for at in range(PARTS)])


def all_exchanged(blocks):
    return [blocks[0]] + [exchanged(blocks[bits], bits) for bits in range(1, PARTS)]


def pack_kernel(place, mask, diffusion, inverse, remap, mine, sent):
    rows, cols = mask.shape
    levels = inverse.shape[0]
    half, wide = levels // 2, cols // PARTS + 2
    wet = mask[...].astype(jnp.float32)
    nothing = jnp.zeros((1, rows), jnp.float32)
    folded = jnp.concatenate([inverse[:half, :], inverse[half:, :]], axis=1)
    for pack, part in ((mine, place[0]), (sent, place[0] ^ 2)):
        for slot, plane in enumerate((wet.T, (wet * diffusion[...]).T)):
            block = jnp.concatenate([nothing, plane, nothing], axis=0)
            for at in range(PARTS):

                @pl.when(part == at)
                def _():
                    first = at * (wide - 2)
                    pack[slot * wide : (slot + 1) * wide, :] = block[first : first + wide]

        pack[2 * wide : 2 * wide + half, :] = folded
        pack[2 * wide + half :, :] = remap[...].astype(jnp.float32)


def parameters(place, mask, diffusion, inverse, remap):
    rows, cols = mask.shape
    count = 2 * (cols // PARTS + 2) + inverse.shape[0] // 2 + 1
    pack = jax.ShapeDtypeStruct((count, rows), jnp.float32)
    return pl.pallas_call(
        pack_kernel,
        out_shape=[pack, pack],
        in_specs=[SMEM] + [VMEM] * 4,
        out_specs=[VMEM, VMEM],
        name="parameters",
    )(place, mask, diffusion, inverse, remap)


def split_kernel(place, field, p0, p1, p2, p3, q2, ends, turned):
    levels, rows, cols = field.shape
    width = cols // PARTS
    turned[0] = jnp.zeros((levels, rows), jnp.float32)
    turned[cols + 1] = jnp.zeros((levels, rows), jnp.float32)
    flat = turned.reshape((cols + 2) * levels, rows)
    for level in range(levels):
        flat[pl.ds(levels + level, cols, stride=levels), :] = field[level].T
    for bits, part in ((0, p0), (1, p1), (2, p2), (3, p3)):
        part[...] = turned[pl.ds((place[0] ^ bits) * width, part.shape[0])]
    q2[...] = turned[pl.ds((place[0] ^ 2) * width + p2.shape[0], q2.shape[0])]
    ends[0] = turned[1]
    ends[1] = turned[cols]


def split_columns(place, field):
    levels, rows, cols = field.shape
    wide = cols // PARTS + 2
    counts = [wide, wide, FIRST, wide, wide - FIRST, 2]
    return pl.pallas_call(
        split_kernel,
        grid=(levels // BLOCK,),
        out_shape=[jax.ShapeDtypeStruct((count, levels, rows), jnp.float32) for count in counts],
        in_specs=[SMEM, pl.BlockSpec((BLOCK, rows, cols), lambda i: (i, 0, 0))],
        out_specs=[pl.BlockSpec((count, BLOCK, rows), lambda i: (0, i, 0)) for count in counts],
        scratch_shapes=[pltpu.VMEM((cols + 2, BLOCK, rows), jnp.float32)],
        name="split_columns",
    )(place, field)


def border_kernel(place, lent_rows, field, ends, gain, borders, held, arrivals):
    levels, rows, cols = field.shape
    wanted = (0, rows - 1, lent_rows[0], lent_rows[rows - 1])
    copies = [
        pltpu.make_async_copy(field.at[:, pl.ds(row, 1), :], held.at[slot], arrivals.at[slot])
        for slot, row in enumerate(wanted)
    ]
    for copy in copies:
        copy.start()
    for copy in copies:
        copy.wait()
    component = place[0] // 2
    for at in range(PARTS):
        lent = (component != at // 2).astype(jnp.int32)
        for slot in range(2):
            borders[at, slot * levels : (slot + 1) * levels, :] = held[2 * lent + slot].reshape(levels, cols)
            borders[at, (2 + slot) * levels : (3 + slot) * levels, :] = ends[slot]
        borders[at, 4 * levels :, :] = jnp.zeros((1, rows), jnp.float32)
        borders[at, 4 * levels :, :levels] = gain[...]


def side_borders(place, lent_rows, field, ends, gain):
    levels, rows, cols = field.shape
    return pl.pallas_call(
        border_kernel,
        out_shape=jax.ShapeDtypeStruct((PARTS, 4 * levels + 1, rows), jnp.float32),
        in_specs=[SMEM, SMEM, pl.BlockSpec(memory_space=pl.ANY), VMEM, VMEM],
        out_specs=VMEM,
        scratch_shapes=[pltpu.VMEM((4, levels, 1, cols), jnp.float32), pltpu.SemaphoreType.DMA((4,))],
        name="side_borders",
    )(place, lent_rows, field, ends, gain)


def join_kernel(place, p0, p1, p2, p3, sides, top_bottom, out, turned):
    levels, rows, cols = out.shape
    width = cols // PARTS
    for bits, part in enumerate((p0, p1, p2, p3)):
        turned[pl.ds((place[0] ^ bits) * width, width)] = part[...]
    for part in range(PARTS):
        for side in range(2):
            at = part * width + side * (width - 1)
            turned[at] = turned[at] + sides[part, side]
    flat = turned.reshape(cols * levels, rows)
    row = lax.broadcasted_iota(jnp.int32, (rows, cols), 0)
    for level in range(levels):
        plane = flat[pl.ds(level, cols, stride=levels), :].T
        top = top_bottom[0, level : level + 1, :]
        bottom = top_bottom[1, level : level + 1, :]
        out[level] = plane + jnp.where(row == 0, top, jnp.where(row == rows - 1, bottom, 0.0))


def join_columns(place, parts, sides, top_bottom):
    width, levels, rows = parts[0].shape
    cols = width * PARTS
    return pl.pallas_call(
        join_kernel,
        grid=(levels // BLOCK,),
        out_shape=jax.ShapeDtypeStruct((levels, rows, cols), jnp.float32),
        in_specs=[SMEM]
        + [pl.BlockSpec((width, BLOCK, rows), lambda i: (0, i, 0))] * PARTS
        + [
            pl.BlockSpec((PARTS, 2, BLOCK, rows), lambda i: (0, 0, i, 0)),
            pl.BlockSpec((2, BLOCK, cols), lambda i: (0, i, 0)),
        ],
        out_specs=pl.BlockSpec((BLOCK, rows, cols), lambda i: (i, 0, 0)),
        scratch_shapes=[pltpu.VMEM((cols, BLOCK, rows), jnp.float32)],
        compiler_params=pltpu.CompilerParams(vmem_limit_bytes=16 << 20),
        name="join_columns",
    )(place, *parts, sides, top_bottom)


def halves(value):
    high = value.astype(jnp.bfloat16)
    low = (value - high.astype(jnp.float32)).astype(jnp.bfloat16)
    return high, low


def picked(value, index):
    return jnp.take_along_axis(value, index, axis=1, mode="promise_in_bounds")


def steps_kernel(
    place, p0, p1, p2, p3, q2, my_pack, other_pack, gains, halos,
    o0, o1, o2, o3, edges, column, state,
):
    outs = (o0, o1, o2, o3)
    wide, half, rows = p0.shape
    spot, width = place[0], wide - 2
    packs = (my_pack, other_pack)
    at_once, few = 16, 8
    levels = 2 * half
    lane = lax.broadcasted_iota(jnp.int32, (levels, rows), 1)
    mixes, picks = [], []
    for pack in packs:
        folded = pack[2 * wide : 2 * wide + half, :].T
        mix = jnp.concatenate([folded[:levels], folded[levels:]], axis=1)
        turned = jnp.concatenate([mix[half:], mix[:half]], axis=0)
        turned = jnp.concatenate([turned[:, half:], turned[:, :half]], axis=1)
        high, low = halves(jnp.where(spot % 2 == 0, mix, turned))
        mixes.append(jnp.concatenate([high, low, high], axis=1))
        pick = pack[2 * wide + half :, :].astype(jnp.int32)
        picks.append(jnp.broadcast_to(pick, (levels, rows)))

    def joined(blocks, comp, *at):
        return jnp.concatenate(
            [blocks[(spot ^ (2 * comp + part),) + at] for part in range(2)], axis=0
        )

    gain = []
    for comp in range(2):
        parts_of = [jnp.broadcast_to(gains[spot ^ (2 * comp + part)], (rows, rows)).T for part in range(2)]
        gain.append(jnp.concatenate([block[:half] for block in parts_of], axis=0))

    def solve(load, first, store, count):
        for comp in range(2):
            rights = []
            for at in range(count):
                coupled = load(comp, first + at)
                coupled = coupled + gain[comp] * picked(load(1 - comp, first + at), picks[comp])
                high, low = halves(coupled)
                rights.append(jnp.concatenate([high, high, low], axis=0))
            for at in range(0, count, 2):
                pair = jnp.concatenate(rights[at : at + 2], axis=1)
                solved = jnp.dot(mixes[comp], pair, preferred_element_type=jnp.float32)
                for side in range(2):
                    column[comp, store + at + side] = solved[:, side * rows : (side + 1) * rows]

    def flux(comp, at):
        return column[comp, at] * packs[comp][pl.ds(wide + at, 1), :]

    def lap(around, ends):
        mid = around[1]
        above = jnp.where(lane == 0, ends, pltpu.roll(mid, 1, 1))
        below = jnp.where(lane == rows - 1, ends, pltpu.roll(mid, rows - 1, 1))
        return above + below + around[0] + around[2] - 4.0 * mid

    def arrived(comp, at):
        if comp == 0:
            blocks = [p0[at], p1[at]]
        else:
            blocks = [p2[at] if at < FIRST else q2[at - FIRST], p3[at]]
        return jnp.concatenate(blocks, axis=0)

    for first in range(0, wide, at_once):
        solve(arrived, first, first, min(at_once, wide - first))
    tops = []
    for comp in range(2):
        folded = [halos[spot ^ (2 * comp + part), half:] for part in range(2)]
        folded = [block[:, first : first + 2 * width] for block in folded for first in (0, 2 * width)]
        ends = jnp.concatenate(folded, axis=0)
        tops.append(jnp.concatenate([ends, ends], axis=1))
    outer = []
    for comp in range(2):
        across = joined(halos, comp, slice(0, half))
        outer.append(
            (
                jnp.where(place[0] == 0, across, flux(comp, 0)),
                jnp.where(place[0] == PARTS - 1, across, flux(comp, width + 1)),
            )
        )

    def spread_first(first, left, right):
        for comp in range(2):
            fluxes = [flux(comp, first + at) for at in range(few + 2)]
            if left:
                fluxes[0] = outer[comp][0]
            if right:
                fluxes[-1] = outer[comp][1]
            for at in range(few):
                j = first + at
                ends = picked(tops[comp], jnp.where(lane == 0, j, j + width))
                total = column[comp, j + 1] + lap(fluxes[at : at + 3], ends)
                state[comp, j] = packs[comp][pl.ds(j + 1, 1), :] * total

    for first in range(0, width, few):
        spread_first(first, first == 0, first + few == width)

    def held(comp, at):
        return state[comp, at]

    for first in range(0, width, at_once):
        solve(held, first, first + 1, at_once)
    for comp in range(2):
        column[comp, 0] = jnp.zeros((levels, rows), jnp.float32)
        column[comp, width + 1] = jnp.zeros((levels, rows), jnp.float32)

    def second_spread(step, carry):
        kept = []
        for comp in range(2):
            first = step * few
            fluxes = [flux(comp, first + at) for at in range(few + 2)]
            both = carry[comp]
            for at in range(few):
                j = first + at
                total = column[comp, j + 1] + lap(fluxes[at : at + 3], 0.0)
                done = packs[comp][pl.ds(j + 1, 1), :] * total
                outs[2 * comp][j] = done[:half]
                outs[2 * comp + 1][j] = done[half:]
                ends = picked(fluxes[at + 1], jnp.where(lane == j, 0, rows - 1))
                both = jnp.where((lane == j) | (lane == j + width), ends, both)
            kept.append(both)
        return tuple(kept)

    empty = jnp.zeros((levels, rows), jnp.float32)
    both = (empty, empty)
    for step in range(width // few):
        both = second_spread(step, both)
    for comp in range(2):
        for part in range(2):
            to, span = spot ^ (2 * comp + part), slice(part * half, (part + 1) * half)
            edges[to, :half] = flux(comp, 1)[span]
            edges[to, half : 2 * half] = flux(comp, width)[span]
            ends = both[comp][span, : 2 * width]
            edges[to, 2 * half :] = jnp.concatenate([ends[: half // 2], ends[half // 2 :]], axis=1)


def two_steps(place, parts, packs, gains, halos):
    wide, half, rows = parts[0].shape
    width = wide - 2
    part = pltpu.HBM((width, half, rows), jnp.float32)
    *results, edges = pl.pallas_call(
        steps_kernel,
        out_shape=[part] * 2 + [pltpu.VMEM((width, half, rows), jnp.float32)] * 2 + [pltpu.VMEM((PARTS, 2 * half + half // 2, rows), jnp.float32)],
        in_specs=[SMEM] + [VMEM] * 9,
        out_specs=[VMEM] * (PARTS + 1),
        scratch_shapes=[
            pltpu.VMEM((2, wide, 2 * half, rows), jnp.float32),
            pltpu.VMEM((2, width, 2 * half, rows), jnp.float32),
        ],
        compiler_params=pltpu.CompilerParams(vmem_limit_bytes=24 << 20),
        name="two_steps",
    )(place, *map(in_vmem, parts), *packs, gains, halos)
    return results, edges


def tile_halo(edges, nbr_tile, nbr_side, nbr_flip):
    every = lax.all_gather(edges, "tile", axis=0)
    found = every[jnp.maximum(nbr_tile, 0), nbr_side]
    turned = jnp.where((nbr_flip == 1)[:, None, None], found[..., ::-1], found)
    return jnp.where((nbr_tile >= 0)[:, None, None], turned, jnp.float32(0.0))


def on_device(
    adjoint, diffusion, wet_mask, remap, coupling, vert_inverse, nbr_tile, nbr_side, nbr_flip
):
    field = adjoint[0, 0]
    half, rows, cols = field.shape
    width = cols // PARTS
    component, level_at = lax.axis_index("sect"), lax.axis_index("lev")
    spot = component * 2 + level_at
    place = spot[None].astype(jnp.int32)
    near = (nbr_tile[0], nbr_side[0], nbr_flip[0])
    inverse = vert_inverse[0, 0]
    my_rows = remap[0, 0]

    own_pack, sent = parameters(place, wet_mask[0, 0], diffusion[0, 0], inverse, remap[0])
    packs = [own_pack, exchanged(sent, 2)]
    other_rows = packs[1][-1].astype(jnp.int32)

    mine, beside, ahead, far, rest, ends = split_columns(place, field)
    ahead = exchanged(ahead, 2)
    borders = side_borders(place, other_rows, field, ends, coupling)
    beside, far, rest, borders, wet_mask, diffusion, inverse = lax.optimization_barrier(
        (beside, far, rest, borders, wet_mask, diffusion, inverse)
    )
    borders = traded(borders)
    parts = [mine, exchanged(beside, 1), ahead, exchanged(far, 3), exchanged(rest, 2)]

    wet = wet_mask[0, 0].astype(jnp.float32)
    spread = wet * diffusion[0, 0]

    gain_rows = borders[:, -1:]
    gains = borders[:, -1, :half].reshape(2, 2 * half)
    borders = borders[:, :-1].reshape(2, 2, 4, half, rows)
    borders = borders.transpose(0, 2, 1, 3, 4).reshape(2, 4, 2 * half, rows)
    own, pulled = [jnp.where(component == comp, borders[0], borders[1]) for comp in range(2)]
    my_gain = jnp.where(component == 0, gains[0], gains[1])
    choose = (jnp.arange(rows)[:, None] == my_rows[None, :]).astype(jnp.float32)
    pulled_columns = jnp.einsum("slq,qr->slr", pulled[2:], choose, precision=HIGHEST)
    coupled = own + my_gain[None, :, None] * jnp.concatenate([pulled[:2], pulled_columns])
    mine = lax.dynamic_slice_in_dim(inverse, level_at * half, half, 1)
    solved = jnp.einsum("kl,skx->slx", mine, coupled, precision=HIGHEST)

    def border(plane):
        return jnp.stack([plane[0], plane[rows - 1], plane[:, 0], plane[:, cols - 1]])[:, None, :]

    halo = tile_halo(solved * border(spread), *near)
    blocks = []
    for part in range(PARTS):
        span = slice(part * width, (part + 1) * width)
        ends = jnp.concatenate([halo[0][:, span], halo[1][:, span]], axis=1)
        ends = jnp.concatenate([ends[: half // 2], ends[half // 2 :]], axis=1)
        blocks.append(jnp.concatenate([halo[2] if part == 0 else halo[3], ends]))
    halos = traded(jnp.stack(blocks))

    results, edges = two_steps(place, parts, packs, gain_rows, halos)

    edges = traded(edges)
    results = all_exchanged(results)
    starts, stops, folded = edges[:, :half], edges[:, half : 2 * half], edges[:, 2 * half :]
    folded = folded.reshape(PARTS, half // 2, 2, 2, width).transpose(3, 2, 1, 0, 4).reshape(2, half, cols)
    halo = tile_halo(jnp.concatenate([folded, starts[:1], stops[PARTS - 1 :]]), *near)
    sides = []
    for part in range(PARTS):
        left = halo[2] if part == 0 else stops[part - 1]
        right = halo[3] if part == PARTS - 1 else starts[part + 1]
        sides.append(
            jnp.stack([left * wet[:, part * width], right * wet[:, (part + 1) * width - 1]])
        )
    top_bottom = jnp.stack([halo[0] * wet[0], halo[1] * wet[rows - 1]])
    return join_columns(place, results, jnp.stack(sides), top_bottom)[None, None]


def solution(mesh):
    in_specs = (
        P("sect", "tile", "lev", None, None),
        P("sect", "tile", None, None),
        P("sect", "tile", None, None),
        P("sect", "tile", None),
        P("sect", "lev"),
        P("sect", "tile", None, None),
        P("tile", None),
        P("tile", None),
        P("tile", None),
    )
    out_specs = P("sect", "tile", "lev", None, None)
    return jax.shard_map(
        on_device, mesh=mesh, in_specs=in_specs, out_specs=out_specs, check_vma=False
    )
```

```python
import jax
import jax.numpy as jnp
from jax import lax
from jax.experimental import pallas as pl
from jax.experimental.pallas import tpu as pltpu
from jax.sharding import PartitionSpec as P

Z = ("sect", "lev")
PARTS = 4
BLOCK = 16
FIRST = 24
HIGHEST = lax.Precision.HIGHEST
SMEM = pl.BlockSpec(memory_space=pltpu.SMEM)
VMEM = pl.BlockSpec(memory_space=pltpu.VMEM)


def in_vmem(block):
    return pltpu.with_memory_space_constraint(block, pltpu.VMEM)


def traded(blocks):
    return lax.all_to_all(blocks, Z, 0, 0)


def exchanged(block, bits):
    return lax.ppermute(block, Z, [(at, at ^ bits) for at in range(PARTS)])


def all_exchanged(blocks):
    return [blocks[0]] + [exchanged(blocks[bits], bits) for bits in range(1, PARTS)]


def pack_kernel(place, mask, diffusion, inverse, remap, mine, sent):
    rows, cols = mask.shape
    levels = inverse.shape[0]
    half, wide = levels // 2, cols // PARTS + 2
    wet = mask[...].astype(jnp.float32)
    nothing = jnp.zeros((1, rows), jnp.float32)
    folded = jnp.concatenate([inverse[:half, :], inverse[half:, :]], axis=1)
    for pack, part in ((mine, place[0]), (sent, place[0] ^ 2)):
        for slot, plane in enumerate((wet.T, (wet * diffusion[...]).T)):
            block = jnp.concatenate([nothing, plane, nothing], axis=0)
            for at in range(PARTS):

                @pl.when(part == at)
                def _():
                    first = at * (wide - 2)
                    pack[slot * wide : (slot + 1) * wide, :] = block[first : first + wide]

        pack[2 * wide : 2 * wide + half, :] = folded
        pack[2 * wide + half :, :] = remap[...].astype(jnp.float32)


def parameters(place, mask, diffusion, inverse, remap):
    rows, cols = mask.shape
    count = 2 * (cols // PARTS + 2) + inverse.shape[0] // 2 + 1
    pack = jax.ShapeDtypeStruct((count, rows), jnp.float32)
    return pl.pallas_call(
        pack_kernel,
        out_shape=[pack, pack],
        in_specs=[SMEM] + [VMEM] * 4,
        out_specs=[VMEM, VMEM],
        name="parameters",
    )(place, mask, diffusion, inverse, remap)


def split_kernel(place, field, p0, p1, p2, p3, q2, ends, turned):
    levels, rows, cols = field.shape
    width = cols // PARTS
    turned[0] = jnp.zeros((levels, rows), jnp.float32)
    turned[cols + 1] = jnp.zeros((levels, rows), jnp.float32)
    flat = turned.reshape((cols + 2) * levels, rows)
    for level in range(levels):
        flat[pl.ds(levels + level, cols, stride=levels), :] = field[level].T
    for bits, part in ((0, p0), (1, p1), (2, p2), (3, p3)):
        part[...] = turned[pl.ds((place[0] ^ bits) * width, part.shape[0])]
    q2[...] = turned[pl.ds((place[0] ^ 2) * width + p2.shape[0], q2.shape[0])]
    ends[0] = turned[1]
    ends[1] = turned[cols]


def split_columns(place, field):
    levels, rows, cols = field.shape
    wide = cols // PARTS + 2
    counts = [wide, wide, FIRST, wide, wide - FIRST, 2]
    return pl.pallas_call(
        split_kernel,
        grid=(levels // BLOCK,),
        out_shape=[jax.ShapeDtypeStruct((count, levels, rows), jnp.float32) for count in counts],
        in_specs=[SMEM, pl.BlockSpec((BLOCK, rows, cols), lambda i: (i, 0, 0))],
        out_specs=[pl.BlockSpec((count, BLOCK, rows), lambda i: (0, i, 0)) for count in counts],
        scratch_shapes=[pltpu.VMEM((cols + 2, BLOCK, rows), jnp.float32)],
        name="split_columns",
    )(place, field)


def border_kernel(place, lent_rows, field, ends, gain, borders, held, arrivals):
    levels, rows, cols = field.shape
    wanted = (0, rows - 1, lent_rows[0], lent_rows[rows - 1])
    copies = [
        pltpu.make_async_copy(field.at[:, pl.ds(row, 1), :], held.at[slot], arrivals.at[slot])
        for slot, row in enumerate(wanted)
    ]
    for copy in copies:
        copy.start()
    for copy in copies:
        copy.wait()
    component = place[0] // 2
    for at in range(PARTS):
        lent = (component != at // 2).astype(jnp.int32)
        for slot in range(2):
            borders[at, slot * levels : (slot + 1) * levels, :] = held[2 * lent + slot].reshape(levels, cols)
            borders[at, (2 + slot) * levels : (3 + slot) * levels, :] = ends[slot]
        borders[at, 4 * levels :, :] = jnp.zeros((1, rows), jnp.float32)
        borders[at, 4 * levels :, :levels] = gain[...]


def side_borders(place, lent_rows, field, ends, gain):
    levels, rows, cols = field.shape
    return pl.pallas_call(
        border_kernel,
        out_shape=jax.ShapeDtypeStruct((PARTS, 4 * levels + 1, rows), jnp.float32),
        in_specs=[SMEM, SMEM, pl.BlockSpec(memory_space=pl.ANY), VMEM, VMEM],
        out_specs=VMEM,
        scratch_shapes=[pltpu.VMEM((4, levels, 1, cols), jnp.float32), pltpu.SemaphoreType.DMA((4,))],
        name="side_borders",
    )(place, lent_rows, field, ends, gain)


def join_kernel(place, p0, p1, p2, p3, sides, top_bottom, out, turned):
    levels, rows, cols = out.shape
    width = cols // PARTS
    for bits, part in enumerate((p0, p1, p2, p3)):
        turned[pl.ds((place[0] ^ bits) * width, width)] = part[...]
    for part in range(PARTS):
        for side in range(2):
            at = part * width + side * (width - 1)
            turned[at] = turned[at] + sides[part, side]
    flat = turned.reshape(cols * levels, rows)
    row = lax.broadcasted_iota(jnp.int32, (rows, cols), 0)
    for level in range(levels):
        plane = flat[pl.ds(level, cols, stride=levels), :].T
        top = top_bottom[0, level : level + 1, :]
        bottom = top_bottom[1, level : level + 1, :]
        out[level] = plane + jnp.where(row == 0, top, jnp.where(row == rows - 1, bottom, 0.0))


def join_columns(place, parts, sides, top_bottom):
    width, levels, rows = parts[0].shape
    cols = width * PARTS
    return pl.pallas_call(
        join_kernel,
        grid=(levels // BLOCK,),
        out_shape=jax.ShapeDtypeStruct((levels, rows, cols), jnp.float32),
        in_specs=[SMEM]
        + [pl.BlockSpec((width, BLOCK, rows), lambda i: (0, i, 0))] * PARTS
        + [
            pl.BlockSpec((PARTS, 2, BLOCK, rows), lambda i: (0, 0, i, 0)),
            pl.BlockSpec((2, BLOCK, cols), lambda i: (0, i, 0)),
        ],
        out_specs=pl.BlockSpec((BLOCK, rows, cols), lambda i: (i, 0, 0)),
        scratch_shapes=[pltpu.VMEM((cols, BLOCK, rows), jnp.float32)],
        compiler_params=pltpu.CompilerParams(vmem_limit_bytes=16 << 20),
        name="join_columns",
    )(place, *parts, sides, top_bottom)


def halves(value):
    high = value.astype(jnp.bfloat16)
    low = (value - high.astype(jnp.float32)).astype(jnp.bfloat16)
    return high, low


def picked(value, index):
    return jnp.take_along_axis(value, index, axis=1, mode="promise_in_bounds")


def steps_kernel(
    place, p0, p1, p2, p3, q2, my_pack, other_pack, gains, halos,
    o0, o1, o2, o3, edges, column, state,
):
    outs = (o0, o1, o2, o3)
    wide, half, rows = p0.shape
    spot, width = place[0], wide - 2
    packs = (my_pack, other_pack)
    at_once, few = 16, 8
    levels = 2 * half
    lane = lax.broadcasted_iota(jnp.int32, (levels, rows), 1)
    mixes, picks = [], []
    for pack in packs:
        folded = pack[2 * wide : 2 * wide + half, :].T
        mix = jnp.concatenate([folded[:levels], folded[levels:]], axis=1)
        turned = jnp.concatenate([mix[half:], mix[:half]], axis=0)
        turned = jnp.concatenate([turned[:, half:], turned[:, :half]], axis=1)
        high, low = halves(jnp.where(spot % 2 == 0, mix, turned))
        mixes.append(jnp.concatenate([high, low, high], axis=1))
        pick = pack[2 * wide + half :, :].astype(jnp.int32)
        picks.append(jnp.broadcast_to(pick, (levels, rows)))

    def joined(blocks, comp, *at):
        return jnp.concatenate(
            [blocks[(spot ^ (2 * comp + part),) + at] for part in range(2)], axis=0
        )

    gain = []
    for comp in range(2):
        parts_of = [jnp.broadcast_to(gains[spot ^ (2 * comp + part)], (rows, rows)).T for part in range(2)]
        gain.append(jnp.concatenate([block[:half] for block in parts_of], axis=0))

    def solve(load, first, store, count):
        for comp in range(2):
            rights = []
            for at in range(count):
                coupled = load(comp, first + at)
                coupled = coupled + gain[comp] * picked(load(1 - comp, first + at), picks[comp])
                high, low = halves(coupled)
                rights.append(jnp.concatenate([high, high, low], axis=0))
            for at in range(0, count, 2):
                pair = jnp.concatenate(rights[at : at + 2], axis=1)
                solved = jnp.dot(mixes[comp], pair, preferred_element_type=jnp.float32)
                for side in range(2):
                    column[comp, store + at + side] = solved[:, side * rows : (side + 1) * rows]

    def flux(comp, at):
        return column[comp, at] * packs[comp][pl.ds(wide + at, 1), :]

    def lap(around, ends):
        mid = around[1]
        above = jnp.where(lane == 0, ends, pltpu.roll(mid, 1, 1))
        below = jnp.where(lane == rows - 1, ends, pltpu.roll(mid, rows - 1, 1))
        return above + below + around[0] + around[2] - 4.0 * mid

    def arrived(comp, at):
        if comp == 0:
            blocks = [p0[at], p1[at]]
        else:
            blocks = [p2[at] if at < FIRST else q2[at - FIRST], p3[at]]
        return jnp.concatenate(blocks, axis=0)

    for first in range(0, wide, at_once):
        solve(arrived, first, first, min(at_once, wide - first))
    tops = []
    for comp in range(2):
        folded = [halos[spot ^ (2 * comp + part), half:] for part in range(2)]
        folded = [block[:, first : first + 2 * width] for block in folded for first in (0, 2 * width)]
        ends = jnp.concatenate(folded, axis=0)
        tops.append(jnp.concatenate([ends, ends], axis=1))
    outer = []
    for comp in range(2):
        across = joined(halos, comp, slice(0, half))
        outer.append(
            (
                jnp.where(place[0] == 0, across, flux(comp, 0)),
                jnp.where(place[0] == PARTS - 1, across, flux(comp, width + 1)),
            )
        )

    def spread_first(first, left, right):
        for comp in range(2):
            fluxes = [flux(comp, first + at) for at in range(few + 2)]
            if left:
                fluxes[0] = outer[comp][0]
            if right:
                fluxes[-1] = outer[comp][1]
            for at in range(few):
                j = first + at
                ends = picked(tops[comp], jnp.where(lane == 0, j, j + width))
                total = column[comp, j + 1] + lap(fluxes[at : at + 3], ends)
                state[comp, j] = packs[comp][pl.ds(j + 1, 1), :] * total

    for first in range(0, width, few):
        spread_first(first, first == 0, first + few == width)

    def held(comp, at):
        return state[comp, at]

    for first in range(0, width, at_once):
        solve(held, first, first + 1, at_once)
    for comp in range(2):
        column[comp, 0] = jnp.zeros((levels, rows), jnp.float32)
        column[comp, width + 1] = jnp.zeros((levels, rows), jnp.float32)

    def second_spread(step, carry):
        kept = []
        for comp in range(2):
            first = step * few
            fluxes = [flux(comp, first + at) for at in range(few + 2)]
            both = carry[comp]
            for at in range(few):
                j = first + at
                total = column[comp, j + 1] + lap(fluxes[at : at + 3], 0.0)
                done = packs[comp][pl.ds(j + 1, 1), :] * total
                outs[2 * comp][j] = done[:half]
                outs[2 * comp + 1][j] = done[half:]
                ends = picked(fluxes[at + 1], jnp.where(lane == j, 0, rows - 1))
                both = jnp.where((lane == j) | (lane == j + width), ends, both)
            kept.append(both)
        return tuple(kept)

    empty = jnp.zeros((levels, rows), jnp.float32)
    both = (empty, empty)
    for step in range(width // few):
        both = second_spread(step, both)
    for comp in range(2):
        for part in range(2):
            to, span = spot ^ (2 * comp + part), slice(part * half, (part + 1) * half)
            edges[to, :half] = flux(comp, 1)[span]
            edges[to, half : 2 * half] = flux(comp, width)[span]
            ends = both[comp][span, : 2 * width]
            edges[to, 2 * half :] = jnp.concatenate([ends[: half // 2], ends[half // 2 :]], axis=1)


def two_steps(place, parts, packs, gains, halos):
    wide, half, rows = parts[0].shape
    width = wide - 2
    part = pltpu.HBM((width, half, rows), jnp.float32)
    *results, edges = pl.pallas_call(
        steps_kernel,
        out_shape=[part] * PARTS + [pltpu.VMEM((PARTS, 2 * half + half // 2, rows), jnp.float32)],
        in_specs=[SMEM] + [VMEM] * 9,
        out_specs=[VMEM] * (PARTS + 1),
        scratch_shapes=[
            pltpu.VMEM((2, wide, 2 * half, rows), jnp.float32),
            pltpu.VMEM((2, width, 2 * half, rows), jnp.float32),
        ],
        compiler_params=pltpu.CompilerParams(vmem_limit_bytes=24 << 20),
        name="two_steps",
    )(place, *map(in_vmem, parts), *packs, gains, halos)
    return results, edges


def tile_halo(edges, nbr_tile, nbr_side, nbr_flip):
    every = lax.all_gather(edges, "tile", axis=0)
    found = every[jnp.maximum(nbr_tile, 0), nbr_side]
    turned = jnp.where((nbr_flip == 1)[:, None, None], found[..., ::-1], found)
    return jnp.where((nbr_tile >= 0)[:, None, None], turned, jnp.float32(0.0))


def on_device(
    adjoint, diffusion, wet_mask, remap, coupling, vert_inverse, nbr_tile, nbr_side, nbr_flip
):
    field = adjoint[0, 0]
    half, rows, cols = field.shape
    width = cols // PARTS
    component, level_at = lax.axis_index("sect"), lax.axis_index("lev")
    spot = component * 2 + level_at
    place = spot[None].astype(jnp.int32)
    near = (nbr_tile[0], nbr_side[0], nbr_flip[0])
    inverse = vert_inverse[0, 0]
    my_rows = remap[0, 0]

    own_pack, sent = parameters(place, wet_mask[0, 0], diffusion[0, 0], inverse, remap[0])
    packs = [own_pack, exchanged(sent, 2)]
    other_rows = packs[1][-1].astype(jnp.int32)

    mine, beside, ahead, far, rest, ends = split_columns(place, field)
    ahead = exchanged(ahead, 2)
    borders = side_borders(place, other_rows, field, ends, coupling)
    beside, far, rest, borders, wet_mask, diffusion, inverse = lax.optimization_barrier(
        (beside, far, rest, borders, wet_mask, diffusion, inverse)
    )
    borders = traded(borders)
    parts = [mine, exchanged(beside, 1), ahead, exchanged(far, 3), exchanged(rest, 2)]

    wet = wet_mask[0, 0].astype(jnp.float32)
    spread = wet * diffusion[0, 0]

    gain_rows = borders[:, -1:]
    gains = borders[:, -1, :half].reshape(2, 2 * half)
    borders = borders[:, :-1].reshape(2, 2, 4, half, rows)
    borders = borders.transpose(0, 2, 1, 3, 4).reshape(2, 4, 2 * half, rows)
    own, pulled = [jnp.where(component == comp, borders[0], borders[1]) for comp in range(2)]
    my_gain = jnp.where(component == 0, gains[0], gains[1])
    choose = (jnp.arange(rows)[:, None] == my_rows[None, :]).astype(jnp.float32)
    pulled_columns = jnp.einsum("slq,qr->slr", pulled[2:], choose, precision=HIGHEST)
    coupled = own + my_gain[None, :, None] * jnp.concatenate([pulled[:2], pulled_columns])
    mine = lax.dynamic_slice_in_dim(inverse, level_at * half, half, 1)
    solved = jnp.einsum("kl,skx->slx", mine, coupled, precision=HIGHEST)

    def border(plane):
        return jnp.stack([plane[0], plane[rows - 1], plane[:, 0], plane[:, cols - 1]])[:, None, :]

    halo = tile_halo(solved * border(spread), *near)
    blocks = []
    for part in range(PARTS):
        span = slice(part * width, (part + 1) * width)
        ends = jnp.concatenate([halo[0][:, span], halo[1][:, span]], axis=1)
        ends = jnp.concatenate([ends[: half // 2], ends[half // 2 :]], axis=1)
        blocks.append(jnp.concatenate([halo[2] if part == 0 else halo[3], ends]))
    halos = traded(jnp.stack(blocks))

    results, edges = two_steps(place, parts, packs, gain_rows, halos)

    edges = traded(edges)
    results = all_exchanged(results)
    starts, stops, folded = edges[:, :half], edges[:, half : 2 * half], edges[:, 2 * half :]
    folded = folded.reshape(PARTS, half // 2, 2, 2, width).transpose(3, 2, 1, 0, 4).reshape(2, half, cols)
    halo = tile_halo(jnp.concatenate([folded, starts[:1], stops[PARTS - 1 :]]), *near)
    sides = []
    for part in range(PARTS):
        left = halo[2] if part == 0 else stops[part - 1]
        right = halo[3] if part == PARTS - 1 else starts[part + 1]
        sides.append(
            jnp.stack([left * wet[:, part * width], right * wet[:, (part + 1) * width - 1]])
        )
    top_bottom = jnp.stack([halo[0] * wet[0], halo[1] * wet[rows - 1]])
    return join_columns(place, results, jnp.stack(sides), top_bottom)[None, None]


def solution(mesh):
    in_specs = (
        P("sect", "tile", "lev", None, None),
        P("sect", "tile", None, None),
        P("sect", "tile", None, None),
        P("sect", "tile", None),
        P("sect", "lev"),
        P("sect", "tile", None, None),
        P("tile", None),
        P("tile", None),
        P("tile", None),
    )
    out_specs = P("sect", "tile", "lev", None, None)
    return jax.shard_map(
        on_device, mesh=mesh, in_specs=in_specs, out_specs=out_specs, check_vma=False
    )
```
